128 devices in a mesh: src: 8 (over z, core), tgt: 16 (over x, y).
Axes of the slice: x: 4, y: 4, z: 4, core: 2. Of those that a mesh axis runs over, the one named last changes fastest.
Arguments:
- src_emb: bfloat16 [32768, 1024], P(('src', 'tgt')), may hold values from 0 to 500, as said below
- tgt_emb: bfloat16 [8192, 1024], P('tgt'), may hold values from 0 to 500, as said below
- pair_list: int32 [128, 8], P('src'), may hold values from 0 to 31, as said below
- fwd_idx: int32 [32768, 16], P('src'), may hold values from 0 to 8191, as said below
- bwd_idx: int32 [8192, 16], P('tgt'), may hold values from 0 to 32767, as said below
Outputs:
- src_best: float32 [32768], P(('src', 'tgt'))
- tgt_best: float32 [8192], P('tgt')
The draws below stay inside these ranges and needn't reach their ends.
Inputs may be any that keep to these rules, and one draw needn't show every extreme that they name: src_emb entries are positive. tgt_emb entries are positive. `pair_list`: each row names 8 distinct target blocks in ascending order. Row b names block c whenever c mod 128 equals b, so every target block is named. All 2 blocks of one tgt index, the same for every row, are named in every row. `fwd_idx`: entry [i, k] is a target row of a block named in row i // 256 of pair_list; entries may repeat. `bwd_idx`: entry [j, k] is a source row of a block whose pair_list row names block j // 256; entries may repeat.
All inputs are finite; a program needn't handle non-finite values.
Results may differ from the reference program's by a relative error of at most 0.00091.
Values may be sent and summed in bfloat16 or wider, within the bound.
A program may use at most 64 MiB of HBM per device.

```python
import jax
import jax.numpy as jnp
from jax import lax

D = 1024
BLOCK = 256
K = 16
P_SIZE = 8
TB_DEV = 2
NSB = 128
NTB = 32
NS = 32768
NT = 8192


def positive_rows(key, count):
    k_scale, k_value, k_band = jax.random.split(key, 3)
    spread = jnp.exp(jax.random.uniform(k_scale, (count, 1), jnp.float32, jnp.log(0.3), jnp.log(1.5)))
    values = jnp.clip(jax.random.normal(k_value, (count, D), jnp.float32), -2.6, 2.6)
    band_pick = jax.random.randint(k_band, (count, 1), 0, 8)
    feature_band = jnp.arange(D, dtype=jnp.int32) // (D // 8)
    boost = jnp.where(feature_band[None, :] == band_pick, 2.0, 0.0).astype(jnp.float32)
    return jnp.exp(spread * values + boost)


def pair_table(key):
    base = jax.random.fold_in(key, 11)
    k_owner, k_rank = jax.random.split(base)
    owner_index = jax.random.randint(k_owner, (), 0, NTB // TB_DEV)
    blocks = jnp.arange(NTB, dtype=jnp.int32)
    popular = (blocks // TB_DEV == owner_index).astype(jnp.int32)
    forced = (blocks[None, :] % NSB == jnp.arange(NSB, dtype=jnp.int32)[:, None]).astype(jnp.int32)
    ranks = jax.vmap(lambda k: jax.random.permutation(k, NTB))(jax.random.split(k_rank, NSB)).astype(jnp.int32)
    scores = ranks + NTB * (forced + 2 * popular[None, :])
    top_scores, chosen = lax.top_k(scores, P_SIZE)
    return jnp.sort(chosen.astype(jnp.int32), axis=1)


def draw_src_emb(key, part):
    return positive_rows(jax.random.fold_in(key, 21), NS).astype(jnp.bfloat16)


def draw_tgt_emb(key, part):
    return positive_rows(jax.random.fold_in(key, 22), NT).astype(jnp.bfloat16)


def draw_pair_list(key, part):
    return pair_table(key)


def draw_fwd_idx(key, part):
    chosen = pair_table(key)
    k_slot, k_inner = jax.random.split(jax.random.fold_in(key, 12))
    slot_pick = jax.random.randint(k_slot, (NS, K), 0, P_SIZE)
    inner_row = jax.random.randint(k_inner, (NS, K), 0, BLOCK)
    home_block = jnp.arange(NS, dtype=jnp.int32) // BLOCK
    return (chosen[home_block[:, None], slot_pick] * BLOCK + inner_row).astype(jnp.int32)


def draw_bwd_idx(key, part):
    chosen = pair_table(key)
    listing = jnp.any(chosen[:, :, None] == jnp.arange(NTB, dtype=jnp.int32)[None, None, :], axis=1).astype(jnp.int32)
    running = jnp.cumsum(listing, axis=0)
    totals = running[NSB - 1]
    k_pick, k_inner = jax.random.split(jax.random.fold_in(key, 13))
    home_block = jnp.arange(NT, dtype=jnp.int32) // BLOCK
    choose = jax.random.randint(k_pick, (NT, K), 0, 1 << 20) % totals[home_block][:, None]
    column = running.T[home_block]
    source_block = jnp.sum((column[:, None, :] <= choose[:, :, None]).astype(jnp.int32), axis=2)
    inner_row = jax.random.randint(k_inner, (NT, K), 0, BLOCK)
    return (source_block * BLOCK + inner_row).astype(jnp.int32)


def setup_inputs(seed: int = 0) -> dict:
    keys = jax.random.split(jax.random.key(seed), 6)
    src_emb = draw_src_emb(jax.random.fold_in(keys[5], 71), 0)
    tgt_emb = draw_tgt_emb(jax.random.fold_in(keys[5], 71), 0)
    pair_list = draw_pair_list(jax.random.fold_in(keys[5], 71), 0)
    fwd_idx = draw_fwd_idx(jax.random.fold_in(keys[5], 71), 0)
    bwd_idx = draw_bwd_idx(jax.random.fold_in(keys[5], 71), 0)
    return {"src_emb": src_emb, "tgt_emb": tgt_emb, "pair_list": pair_list, "fwd_idx": fwd_idx, "bwd_idx": bwd_idx}


def unit_rows(values):
    wide = values.astype(jnp.float32)
    factor = lax.rsqrt(lax.optimization_barrier(jnp.sum(wide * wide, axis=1, keepdims=True)) + 1e-06)
    return (wide * factor).astype(jnp.bfloat16)

def reference(src_emb, tgt_emb, pair_list, fwd_idx, bwd_idx):
    src_unit = unit_rows(src_emb)
    tgt_unit = unit_rows(tgt_emb)
    src_blocks = src_unit.reshape(NSB, BLOCK, D)
    tgt_blocks = tgt_unit.reshape(NTB, BLOCK, D)

    def fwd_block(args):
        block_rows, near_rows = args
        near_vecs = tgt_unit[near_rows].astype(jnp.float32)
        return lax.optimization_barrier(jnp.sum(near_vecs * block_rows.astype(jnp.float32)[:, None, :], axis=(1, 2))) / K

    def bwd_block(args):
        block_rows, near_rows = args
        near_vecs = src_unit[near_rows].astype(jnp.float32)
        return lax.optimization_barrier(jnp.sum(near_vecs * block_rows.astype(jnp.float32)[:, None, :], axis=(1, 2))) / K
    fwd_mean = lax.map(fwd_block, (src_blocks, fwd_idx.reshape(NSB, BLOCK, K)))
    bwd_mean = lax.map(bwd_block, (tgt_blocks, bwd_idx.reshape(NTB, BLOCK, K)))

    def margins(carry, args):
        block_rows, listed, fwd_rows = args
        columns = tgt_blocks[listed].reshape(P_SIZE * BLOCK, D)
        scores = jnp.dot(block_rows, columns.T, preferred_element_type=jnp.float32)
        bwd_cols = bwd_mean[listed].reshape(P_SIZE * BLOCK)
        ratio = 2.0 * scores / (fwd_rows[:, None] + bwd_cols[None, :])
        carry = carry.at[listed].max(lax.optimization_barrier(jnp.max(ratio, axis=0)).reshape(P_SIZE, BLOCK))
        return (carry, lax.optimization_barrier(jnp.max(ratio, axis=1)))
    tgt_peak, src_peak = lax.scan(margins, jnp.zeros((NTB, BLOCK), jnp.float32), (src_blocks, pair_list, fwd_mean))
    return (src_peak.reshape(NS), tgt_peak.reshape(NT))
```

```python
import jax
import jax.numpy as jnp
from jax import lax
from jax.experimental import pallas as pl
from jax.experimental.pallas import tpu as pltpu
from jax.sharding import PartitionSpec as P

D = 1024
MESH = pl.DeviceIdType.MESH
F32 = jnp.float32
BF16 = jnp.bfloat16
I32 = jnp.int32

ROW_REL = (0, 0, 3, 1, 3, 1, 2, 2)
COL_SLOT = ((0, 0), (0, 0), (0, 1), (0, 1), (3, 0), (1, 0), (3, 1), (1, 1),
            (3, 0), (1, 0), (3, 1), (1, 1), (2, 0), (2, 1), (2, 0), (2, 1))


def aligned(value, step):
    return pl.multiple_of(value, step)


def kernel(src_hbm, tgt_hbm, pair_ref, fwd_hbm, bwd_hbm, src_out, tgt_out,
           src_raw, tgt_raw, src_buf, tgt_buf, scores, fwd_raw, bwd_raw, fwd_pos, bwd_pos,
           fwd_val, bwd_val, weight, frow, fcol, brow, fwd_part, fwd_in, bwd_part, bwd_zin,
           bwd_two, bwd_xin, src_part, src_in, tgt_part, tgt_xin, tgt_two, tgt_zin,
           load_sem, send_sem, recv_sem):
    s = lax.axis_index("src")
    t = lax.axis_index("tgt")
    core = lax.rem(s, 2)
    z = s // 2
    x = t // 4
    y = lax.rem(t, 4)

    def y_dev(d):
        return (s, 4 * x + lax.rem(y + d, 4))

    def x_dev(d):
        return (s, 4 * lax.rem(x + d, 4) + y)

    def zc_dev(d):
        dz, dc = d // 2, d % 2
        return (2 * lax.rem(z + dz, 4) + lax.rem(core + dc, 2), t)

    src_load = pltpu.make_async_copy(src_hbm, src_raw, load_sem.at[0])
    src_load.start()
    tgt_load = pltpu.make_async_copy(tgt_hbm, tgt_raw, load_sem.at[1])
    tgt_load.start()
    bwd_load = pltpu.make_async_copy(bwd_hbm, bwd_raw.at[0], load_sem.at[2])
    bwd_load.start()
    fwd_load = pltpu.make_async_copy(
        fwd_hbm.at[:, pl.ds(aligned(x * 1024, 1024), 1024)], fwd_raw, load_sem.at[3])
    fwd_load.start()

    barrier = pltpu.get_barrier_semaphore()
    for d in (1, 2, 3):
        pl.semaphore_signal(barrier, inc=1, device_id=y_dev(d), device_id_type=MESH)
        pl.semaphore_signal(barrier, inc=1, device_id=x_dev(d), device_id_type=MESH)
    for d in range(1, 8):
        pl.semaphore_signal(barrier, inc=1, device_id=zc_dev(d), device_id_type=MESH)

    def remote(src, dst, sem, device):
        return pltpu.make_async_remote_copy(
            src_ref=src, dst_ref=dst, send_sem=send_sem.at[sem], recv_sem=recv_sem.at[sem],
            device_id=device, device_id_type=MESH)

    def normalise(raw, buf, raw_first, buf_first, count):
        def step(i, _):
            wide = raw[pl.ds(aligned(raw_first + i * 16, 16), 16), :].astype(F32)
            factor = lax.rsqrt(jnp.sum(wide * wide, axis=1, keepdims=True) + 1e-06)
            buf[pl.ds(aligned(buf_first + i * 16, 16), 16), :] = (wide * factor).astype(BF16)
            return 0
        lax.fori_loop(0, count // 16, step, 0, unroll=4)

    c256 = core * 256
    c128 = core * 128
    src_load.wait()
    normalise(src_raw, src_buf, 0, 0, 256)
    tgt_load.wait()
    normalise(tgt_raw, tgt_buf, c256, c256, 256)
    pl.semaphore_wait(barrier, 13)

    def srow(first, count):
        return src_buf.at[pl.ds(first, count), :]

    def trow(first, count, step=64):
        return tgt_buf.at[pl.ds(aligned(first, step), count), :]

    own_copies = (
        remote(srow(0, 128), srow(256, 128), 0, y_dev(1)),
        remote(srow(128, 128), srow(384, 128), 1, y_dev(3)),
        remote(trow(c256, 128), trow(512 + c256, 128), 2, x_dev(1)),
        remote(trow(c256 + 128, 128), trow(640 + c256, 128), 3, x_dev(3)),
        remote(srow(128, 128), srow(512, 128), 4, y_dev(1)),
        remote(srow(0, 128), srow(640, 128), 5, y_dev(3)),
        remote(trow(c256 + 128, 128), trow(1024 + c256, 128), 6, x_dev(1)),
        remote(trow(c256, 128), trow(1152 + c256, 128), 7, x_dev(3)),
    )
    idx_copies = (
        remote(bwd_hbm, bwd_raw.at[3], 8, x_dev(1)),
        remote(bwd_hbm, bwd_raw.at[1], 9, x_dev(3)),
        remote(bwd_hbm, bwd_raw.at[2], 10, x_dev(2)),
    )
    for copy in own_copies[:4]:
        copy.start()
    for copy in idx_copies:
        copy.start()
    for copy in own_copies[4:]:
        copy.start()

    normalise(tgt_raw, tgt_buf, 256 - c256, 256 - c256, 256)

    def weight_row(rel, _):
        row = 4 * x + lax.rem(y + rel, 4)
        names = [pair_ref[k, row] for k in range(8)]
        for relx in range(4):
            for p in range(2):
                block = 2 * (4 * lax.rem(x + relx, 4) + y) + p
                hit = jnp.int32(0)
                for k in range(8):
                    hit = hit + jnp.where(names[k] == block, 1, 0)
                value = jnp.full((1, 128), jnp.where(hit > 0, 2.0, 0.0), F32)
                for chunk in range(16):
                    if COL_SLOT[chunk] == (relx, p):
                        weight[rel, :, chunk * 128:(chunk + 1) * 128] = value
        return 0

    lax.fori_loop(0, 4, weight_row, 0)

    lane = lax.broadcasted_iota(I32, (16, 128), 1)

    def far(first, second):
        return jnp.where(lane < 64, first, second), jnp.where(lane < 64, second, first)

    fwd_load.wait()
    fwd_pos[...] = jnp.full((1024, 128), -1, I32)

    def fwd_half(rel, half):
        return fwd_raw[:, pl.ds(aligned(lax.rem(y + rel, 4) * 256 + half * 128, 128), 128)]

    f6, f7 = far(fwd_half(2, 0), fwd_half(2, 1))
    fwd_chunks = (fwd_half(0, 0), fwd_half(0, 1), fwd_half(3, 0), fwd_half(1, 1),
                  fwd_half(3, 1), fwd_half(1, 0), f6, f7)
    for chunk, index in enumerate(fwd_chunks):
        block = index >> 8
        inner = index & 255
        p = block & 1
        rel = ((block >> 3) - x) & 3
        upper = inner >= 128
        near = jnp.where(upper == (rel == 1), 512, jnp.where(rel == 1, 1152, 896))
        quarter = inner >> 6
        distant = jnp.where(quarter == 0, 1536, jnp.where(quarter == 3, 1408,
                            jnp.where(quarter == 2, 1664, 1792))) - p * 128
        base = jnp.where(rel == 0, 0, jnp.where(rel == 2, distant, near))
        column = jnp.where(((block >> 1) & 3) == y, base + p * 256 + inner, -1)
        fwd_pos[chunk * 128:(chunk + 1) * 128, 0:16] = jnp.transpose(column)

    def bwd_rows(index):
        block = index >> 8
        inner = index & 255
        rel = ((block & 3) - y) & 3
        upper = inner >= 128
        near = jnp.where(upper == (rel == 1), 256, jnp.where(rel == 1, 640, 384))
        quarter = inner >> 6
        distant = jnp.where(quarter == 0, 768, jnp.where(quarter == 3, 640,
                            jnp.where(quarter == 2, 768, 896)))
        base = jnp.where(rel == 0, 0, jnp.where(rel == 2, distant, near))
        hit = (block >> 2) == s * 4 + x
        return jnp.where(hit, base + inner, -1)

    def bwd_put(chunk, index):
        bwd_pos[:, chunk * 128:(chunk + 1) * 128] = bwd_rows(index)

    def bwd_half(rel, p, half):
        first = p * 256 + half * 128
        return bwd_raw[rel, :, first:first + 128]

    bwd_load.wait()
    for chunk in range(4):
        bwd_put(chunk, bwd_half(0, chunk // 2, chunk % 2))

    fwd_val[...] = jnp.zeros((1024, 128), F32)
    bwd_val[...] = jnp.zeros((16, 2048), F32)

    def region(row, rows, col, cols):
        def dots(i, _):
            at = pl.ds(aligned(col + i * 256, 256), 256)
            scores[row:row + rows, at] = lax.dot_general(
                src_buf[row:row + rows, :], tgt_buf[at, :], (((1,), (1,)), ((), ())),
                preferred_element_type=F32)
            return 0
        lax.fori_loop(0, cols // 256, dots, 0)

        def fwd_rows(g, _):
            at = pl.ds(aligned(row + g * 8, 8), 8)
            index = fwd_pos[at, :]
            pick = index & 127
            where = index >> 7
            value = fwd_val[at, :]
            for chunk in range(col // 128, (col + cols) // 128):
                found = jnp.take_along_axis(
                    scores[at, chunk * 128:(chunk + 1) * 128], pick, axis=1,
                    mode="promise_in_bounds")
                value = jnp.where(where == chunk, found, value)
            fwd_val[at, :] = value
            return 0
        lax.fori_loop(0, rows // 8, fwd_rows, 0, unroll=4)

        def bwd_cols(i, _):
            at = pl.ds(aligned(col + i * 128, 128), 128)
            index0, index1 = bwd_pos[0:8, at], bwd_pos[8:16, at]
            pick0, pick1 = index0 & 7, index1 & 7
            where0, where1 = index0 >> 3, index1 >> 3

            def group(g, values):
                value0, value1 = values
                here = row // 8 + g
                part = scores[pl.ds(aligned(row + g * 8, 8), 8), at]
                found0 = jnp.take_along_axis(part, pick0, axis=0, mode="promise_in_bounds")
                found1 = jnp.take_along_axis(part, pick1, axis=0, mode="promise_in_bounds")
                return (jnp.where(where0 == here, found0, value0),
                        jnp.where(where1 == here, found1, value1))
            value0, value1 = lax.fori_loop(
                0, rows // 8, group, (bwd_val[0:8, at], bwd_val[8:16, at]), unroll=16)
            bwd_val[0:8, at] = value0
            bwd_val[8:16, at] = value1
            return 0
        lax.fori_loop(0, cols // 128, bwd_cols, 0)

    region(0, 256, 0, 512)

    for copy in own_copies[:4]:
        copy.wait_recv()
    far_copies = (
        remote(srow(256, 64), srow(768, 64), 11, y_dev(1)),
        remote(srow(448, 64), srow(832, 64), 12, y_dev(3)),
        remote(trow(512 + c256, 64), trow(1536 + c128, 64), 13, x_dev(1)),
        remote(trow(704 + c256, 64), trow(1600 + c128, 64), 14, x_dev(3)),
        remote(srow(320, 64), srow(960, 64), 15, y_dev(1)),
        remote(srow(384, 64), srow(896, 64), 16, y_dev(3)),
        remote(trow(576 + c256, 64), trow(1856 + c128, 64), 17, x_dev(1)),
        remote(trow(640 + c256, 64), trow(1792 + c128, 64), 18, x_dev(3)),
    )
    for copy in far_copies:
        copy.start()
    partner = zc_dev(1)
    pass_copies = (
        remote(trow(512 + c256, 256), trow(512 + c256, 256), 19, partner),
        remote(trow(1024 + c256, 256), trow(1024 + c256, 256), 20, partner),
        remote(trow(1536 + c128, 128), trow(1536 + c128, 128), 21, partner),
        remote(trow(1792 + c128, 128), trow(1792 + c128, 128), 22, partner),
    )
    pass_copies[0].start()
    for copy in idx_copies:
        copy.wait_recv()
    for p in range(2):
        bwd_put(4 + 2 * p, bwd_half(3, p, 0))
        bwd_put(5 + 2 * p, bwd_half(1, p, 1))
        bwd_put(8 + 2 * p, bwd_half(3, p, 1))
        bwd_put(9 + 2 * p, bwd_half(1, p, 0))
        near, distant = far(bwd_half(2, p, 0), bwd_half(2, p, 1))
        bwd_put(12 + p, near)
        bwd_put(14 + p, distant)
    pass_copies[0].wait_recv()
    region(0, 256, 512, 512)
    region(256, 256, 0, 1024)

    for copy in own_copies[4:]:
        copy.wait_recv()
    pass_copies[1].start()
    region(512, 256, 0, 1024)
    pass_copies[1].wait_recv()
    region(0, 768, 1024, 512)

    for copy in far_copies[:4]:
        copy.wait_recv()
    pass_copies[2].start()
    region(768, 128, 0, 1536)
    pass_copies[2].wait_recv()
    region(0, 896, 1536, 256)

    for copy in far_copies[4:]:
        copy.wait_recv()
    pass_copies[3].start()
    region(896, 128, 0, 1792)
    pass_copies[3].wait_recv()
    region(0, 1024, 1792, 256)

    lane1 = lane[0:1, :]

    def bwd_sum(chunk):
        return jnp.sum(bwd_val[:, chunk * 128:(chunk + 1) * 128], axis=0, keepdims=True)

    def unfar(first, second):
        return jnp.where(lane1 < 64, first, second), jnp.where(lane1 < 64, second, first)

    def natural_cols(get):
        blocks = [[None] * 4 for _ in range(4)]
        for chunk in range(4):
            blocks[0][chunk] = get(chunk)
        for p in range(2):
            blocks[3][2 * p] = get(4 + 2 * p)
            blocks[1][2 * p + 1] = get(5 + 2 * p)
            blocks[3][2 * p + 1] = get(8 + 2 * p)
            blocks[1][2 * p] = get(9 + 2 * p)
            blocks[2][2 * p], blocks[2][2 * p + 1] = unfar(get(12 + p), get(14 + p))
        return blocks

    def natural_rows(get):
        blocks = [[None] * 2 for _ in range(4)]
        blocks[0] = [get(0), get(1)]
        blocks[3] = [get(2), get(4)]
        blocks[1] = [get(5), get(3)]
        blocks[2] = list(unfar(get(6), get(7)))
        return blocks

    for rel, rows in enumerate(natural_cols(bwd_sum)):
        for i, value in enumerate(rows):
            bwd_part[lax.rem(x + rel, 4), i:i + 1, :] = value
    bwd_z = [remote(bwd_part, bwd_zin.at[d - 1], 22 + d, zc_dev(d)) for d in range(1, 8)]
    for copy in bwd_z:
        copy.start()

    def fwd_sum(chunk):
        values = jnp.transpose(fwd_val[chunk * 128:(chunk + 1) * 128, :])
        return jnp.sum(values[0:16, :], axis=0, keepdims=True)

    for rel, rows in enumerate(natural_rows(fwd_sum)):
        for i, value in enumerate(rows):
            fwd_part[lax.rem(y + rel, 4), i:i + 1, :] = value
    fwd_y = [remote(fwd_part, fwd_in.at[d - 1], 29 + d, y_dev(d)) for d in range(1, 4)]
    for copy in fwd_y:
        copy.start()

    for copy in bwd_z:
        copy.wait_recv()
    total = bwd_part[...]
    for d in range(7):
        total = total + bwd_zin[d]
    bwd_two[...] = total
    bwd_x = [remote(bwd_two, bwd_xin.at[d - 1], 32 + d, x_dev(d)) for d in range(1, 4)]
    for copy in bwd_x:
        copy.start()

    for copy in fwd_y:
        copy.wait_recv()
    frow[...] = (fwd_part[...] + fwd_in[0] + fwd_in[1] + fwd_in[2]) * (1.0 / 16)

    def fwd_mean(rel, half):
        return frow[lax.rem(y + rel, 4), half:half + 1, :]

    m6, m7 = unfar(fwd_mean(2, 0), fwd_mean(2, 1))
    for chunk, row in enumerate((fwd_mean(0, 0), fwd_mean(0, 1), fwd_mean(3, 0), fwd_mean(1, 1),
                                 fwd_mean(3, 1), fwd_mean(1, 0), m6, m7)):
        fcol[chunk * 128:(chunk + 1) * 128, :] = jnp.transpose(jnp.broadcast_to(row, (128, 128)))

    for copy in bwd_x:
        copy.wait_recv()
    bwd_two2 = (bwd_two[...] + bwd_xin[0] + bwd_xin[1] + bwd_xin[2]) * (1.0 / 16)
    bwd_part2 = tgt_part
    bwd_part2[...] = bwd_two2

    def bwd_mean(rel, i):
        return bwd_part2[lax.rem(x + rel, 4), i:i + 1, :]

    def put_brow(chunk, value):
        brow[:, chunk * 128:(chunk + 1) * 128] = value

    for chunk in range(4):
        put_brow(chunk, bwd_mean(0, chunk))
    for p in range(2):
        put_brow(4 + 2 * p, bwd_mean(3, 2 * p))
        put_brow(5 + 2 * p, bwd_mean(1, 2 * p + 1))
        put_brow(8 + 2 * p, bwd_mean(3, 2 * p + 1))
        put_brow(9 + 2 * p, bwd_mean(1, 2 * p))
        near, distant = unfar(bwd_mean(2, 2 * p), bwd_mean(2, 2 * p + 1))
        put_brow(12 + p, near)
        put_brow(14 + p, distant)

    peaks = (jnp.zeros((8, 128), F32),) * 16
    for chunk_row in range(8):
        rel = ROW_REL[chunk_row]

        def margin_rows(g, peaks):
            at = pl.ds(aligned(chunk_row * 128 + g * 8, 8), 8)
            mean = fcol[at, :]
            best = jnp.zeros((8, 128), F32)
            new = []
            for chunk in range(16):
                cols = slice(chunk * 128, (chunk + 1) * 128)
                margin = (scores[at, cols] * weight[rel, :, cols]) / (mean + brow[:, cols])
                best = jnp.maximum(best, margin)
                new.append(jnp.maximum(peaks[chunk], margin))
            fwd_val[at, :] = best
            return tuple(new)

        peaks = lax.fori_loop(0, 16, margin_rows, peaks, unroll=2)

    def tgt_peak(chunk):
        return jnp.max(peaks[chunk], axis=0, keepdims=True)

    for rel, rows in enumerate(natural_cols(tgt_peak)):
        for i, value in enumerate(rows):
            tgt_part[lax.rem(x + rel, 4), i:i + 1, :] = value
    tgt_x = [remote(tgt_part.at[lax.rem(x + d, 4)], tgt_xin.at[d - 1], 35 + d, x_dev(d))
             for d in range(1, 4)]
    for copy in tgt_x:
        copy.start()

    def src_peak(chunk):
        values = jnp.transpose(fwd_val[chunk * 128:(chunk + 1) * 128, :])
        return jnp.max(values, axis=0, keepdims=True)

    for rel, rows in enumerate(natural_rows(src_peak)):
        for i, value in enumerate(rows):
            src_part[lax.rem(y + rel, 4), i:i + 1, :] = value
    src_y = [remote(src_part.at[lax.rem(y + d, 4)], src_in.at[d - 1], 38 + d, y_dev(d))
             for d in range(1, 4)]
    for copy in src_y:
        copy.start()

    for copy in tgt_x:
        copy.wait_recv()
    tgt_two[...] = jnp.maximum(jnp.maximum(tgt_part[x], tgt_xin[0]),
                               jnp.maximum(tgt_xin[1], tgt_xin[2]))
    tgt_z = [remote(tgt_two, tgt_zin.at[d - 1], 41 + d, zc_dev(d)) for d in range(1, 8)]
    for copy in tgt_z:
        copy.start()
    for copy in src_y:
        copy.wait_recv()
    src_out[...] = jnp.maximum(jnp.maximum(src_part[y], src_in[0]),
                               jnp.maximum(src_in[1], src_in[2]))
    for copy in tgt_z:
        copy.wait_recv()
    best = tgt_two[...]
    for d in range(7):
        best = jnp.maximum(best, tgt_zin[d])
    tgt_out[...] = best

    for copies in (own_copies, idx_copies, far_copies, pass_copies, bwd_z, fwd_y, bwd_x,
                   tgt_x, src_y, tgt_z):
        for copy in copies:
            copy.wait_send()


def body(src_emb, tgt_emb, pair_list, fwd_idx, bwd_idx):
    hbm = pl.BlockSpec(memory_space=pl.ANY)
    vmem = pl.BlockSpec(memory_space=pltpu.VMEM)
    src_best, tgt_best = pl.pallas_call(
        kernel,
        out_shape=(jax.ShapeDtypeStruct((2, 128), F32), jax.ShapeDtypeStruct((4, 128), F32)),
        in_specs=[hbm, hbm, pl.BlockSpec(memory_space=pltpu.SMEM), hbm, hbm],
        out_specs=(vmem, vmem),
        scratch_shapes=[
            pltpu.VMEM((256, D), BF16), pltpu.VMEM((512, D), BF16),
            pltpu.VMEM((1024, D), BF16), pltpu.VMEM((2048, D), BF16),
            pltpu.VMEM((1024, 2048), F32),
            pltpu.VMEM((16, 1024), I32), pltpu.VMEM((4, 16, 512), I32),
            pltpu.VMEM((1024, 128), I32), pltpu.VMEM((16, 2048), I32),
            pltpu.VMEM((1024, 128), F32), pltpu.VMEM((16, 2048), F32),
            pltpu.VMEM((4, 1, 2048), F32),
            pltpu.VMEM((4, 2, 128), F32), pltpu.VMEM((1024, 128), F32),
            pltpu.VMEM((1, 2048), F32),
            pltpu.VMEM((4, 2, 128), F32), pltpu.VMEM((3, 4, 2, 128), F32),
            pltpu.VMEM((4, 4, 128), F32), pltpu.VMEM((7, 4, 4, 128), F32),
            pltpu.VMEM((4, 4, 128), F32), pltpu.VMEM((3, 4, 4, 128), F32),
            pltpu.VMEM((4, 2, 128), F32), pltpu.VMEM((3, 2, 128), F32),
            pltpu.VMEM((4, 4, 128), F32), pltpu.VMEM((3, 4, 128), F32),
            pltpu.VMEM((4, 128), F32), pltpu.VMEM((7, 4, 128), F32),
            pltpu.SemaphoreType.DMA((4,)),
            pltpu.SemaphoreType.DMA((49,)), pltpu.SemaphoreType.DMA((49,)),
        ],
        compiler_params=pltpu.CompilerParams(
            collective_id=0, has_side_effects=True, vmem_limit_bytes=60 << 20),
    )(src_emb, tgt_emb, pair_list.T, fwd_idx.T, bwd_idx.T)
    return src_best.reshape(256), tgt_best.reshape(512)


def solution(mesh):
    return jax.shard_map(
        body,
        mesh=mesh,
        in_specs=(
            P(("src", "tgt"), None),
            P("tgt", None),
            P("src", None),
            P("src", None),
            P("tgt", None),
        ),
        out_specs=(P(("src", "tgt")), P("tgt")),
        check_vma=False,
    )
```

```python
import jax
import jax.numpy as jnp
from jax import lax
from jax.experimental import pallas as pl
from jax.experimental.pallas import tpu as pltpu
from jax.sharding import PartitionSpec as P

D = 1024
MESH = pl.DeviceIdType.MESH
F32 = jnp.float32
BF16 = jnp.bfloat16
I32 = jnp.int32

ROW_REL = (0, 0, 3, 1, 3, 1, 2, 2)
COL_SLOT = ((0, 0), (0, 0), (0, 1), (0, 1), (3, 0), (1, 0), (3, 1), (1, 1),
            (3, 0), (1, 0), (3, 1), (1, 1), (2, 0), (2, 1), (2, 0), (2, 1))


def aligned(value, step):
    return pl.multiple_of(value, step)


def kernel(src_hbm, tgt_hbm, pair_ref, fwd_hbm, bwd_hbm, src_out, tgt_out,
           src_raw, tgt_raw, src_buf, tgt_buf, scores, fwd_raw, bwd_raw, fwd_pos, bwd_pos,
           fwd_val, bwd_val, weight, frow, fcol, brow, fwd_part, fwd_in, bwd_part, bwd_zin,
           bwd_two, bwd_xin, src_part, src_in, tgt_part, tgt_xin, tgt_two, tgt_zin,
           load_sem, send_sem, recv_sem):
    s = lax.axis_index("src")
    t = lax.axis_index("tgt")
    core = lax.rem(s, 2)
    z = s // 2
    x = t // 4
    y = lax.rem(t, 4)

    def y_dev(d):
        return (s, 4 * x + lax.rem(y + d, 4))

    def x_dev(d):
        return (s, 4 * lax.rem(x + d, 4) + y)

    def zc_dev(d):
        dz, dc = d // 2, d % 2
        return (2 * lax.rem(z + dz, 4) + lax.rem(core + dc, 2), t)

    src_load = pltpu.make_async_copy(src_hbm, src_raw, load_sem.at[0])
    src_load.start()
    tgt_load = pltpu.make_async_copy(tgt_hbm, tgt_raw, load_sem.at[1])
    tgt_load.start()
    bwd_load = pltpu.make_async_copy(bwd_hbm, bwd_raw.at[0], load_sem.at[2])
    bwd_load.start()
    fwd_load = pltpu.make_async_copy(
        fwd_hbm.at[:, pl.ds(aligned(x * 1024, 1024), 1024)], fwd_raw, load_sem.at[3])
    fwd_load.start()

    barrier = pltpu.get_barrier_semaphore()
    for d in (1, 2, 3):
        pl.semaphore_signal(barrier, inc=1, device_id=y_dev(d), device_id_type=MESH)
        pl.semaphore_signal(barrier, inc=1, device_id=x_dev(d), device_id_type=MESH)
    for d in range(1, 8):
        pl.semaphore_signal(barrier, inc=1, device_id=zc_dev(d), device_id_type=MESH)

    def remote(src, dst, sem, device):
        return pltpu.make_async_remote_copy(
            src_ref=src, dst_ref=dst, send_sem=send_sem.at[sem], recv_sem=recv_sem.at[sem],
            device_id=device, device_id_type=MESH)

    def normalise(raw, buf, raw_first, buf_first, count):
        def step(i, _):
            wide = raw[pl.ds(aligned(raw_first + i * 16, 16), 16), :].astype(F32)
            factor = lax.rsqrt(jnp.sum(wide * wide, axis=1, keepdims=True) + 1e-06)
            buf[pl.ds(aligned(buf_first + i * 16, 16), 16), :] = (wide * factor).astype(BF16)
            return 0
        lax.fori_loop(0, count // 16, step, 0, unroll=4)

    c256 = core * 256
    c128 = core * 128
    src_load.wait()
    normalise(src_raw, src_buf, 0, 0, 256)
    tgt_load.wait()
    normalise(tgt_raw, tgt_buf, c256, c256, 256)
    pl.semaphore_wait(barrier, 13)

    def srow(first, count):
        return src_buf.at[pl.ds(first, count), :]

    def trow(first, count, step=64):
        return tgt_buf.at[pl.ds(aligned(first, step), count), :]

    own_copies = (
        remote(srow(0, 128), srow(256, 128), 0, y_dev(1)),
        remote(srow(128, 128), srow(384, 128), 1, y_dev(3)),
        remote(trow(c256, 128), trow(512 + c256, 128), 2, x_dev(1)),
        remote(trow(c256 + 128, 128), trow(640 + c256, 128), 3, x_dev(3)),
        remote(srow(128, 128), srow(512, 128), 4, y_dev(1)),
        remote(srow(0, 128), srow(640, 128), 5, y_dev(3)),
        remote(trow(c256 + 128, 128), trow(1024 + c256, 128), 6, x_dev(1)),
        remote(trow(c256, 128), trow(1152 + c256, 128), 7, x_dev(3)),
    )
    idx_copies = (
        remote(bwd_hbm, bwd_raw.at[3], 8, x_dev(1)),
        remote(bwd_hbm, bwd_raw.at[1], 9, x_dev(3)),
        remote(bwd_hbm, bwd_raw.at[2], 10, x_dev(2)),
    )
    for copy in own_copies[:4]:
        copy.start()
    for copy in idx_copies:
        copy.start()
    for copy in own_copies[4:]:
        copy.start()

    normalise(tgt_raw, tgt_buf, 256 - c256, 256 - c256, 256)

    def weight_row(rel, _):
        row = 4 * x + lax.rem(y + rel, 4)
        names = [pair_ref[k, row] for k in range(8)]
        for relx in range(4):
            for p in range(2):
                block = 2 * (4 * lax.rem(x + relx, 4) + y) + p
                hit = jnp.int32(0)
                for k in range(8):
                    hit = hit + jnp.where(names[k] == block, 1, 0)
                value = jnp.full((1, 128), jnp.where(hit > 0, 2.0, 0.0), F32)
                for chunk in range(16):
                    if COL_SLOT[chunk] == (relx, p):
                        weight[rel, :, chunk * 128:(chunk + 1) * 128] = value
        return 0

    lax.fori_loop(0, 4, weight_row, 0)

    lane = lax.broadcasted_iota(I32, (16, 128), 1)

    def far(first, second):
        return jnp.where(lane < 64, first, second), jnp.where(lane < 64, second, first)

    fwd_load.wait()
    fwd_pos[...] = jnp.full((1024, 128), -1, I32)

    def fwd_half(rel, half):
        return fwd_raw[:, pl.ds(aligned(lax.rem(y + rel, 4) * 256 + half * 128, 128), 128)]

    f6, f7 = far(fwd_half(2, 0), fwd_half(2, 1))
    fwd_chunks = (fwd_half(0, 0), fwd_half(0, 1), fwd_half(3, 0), fwd_half(1, 1),
                  fwd_half(3, 1), fwd_half(1, 0), f6, f7)
    for chunk, index in enumerate(fwd_chunks):
        block = index >> 8
        inner = index & 255
        p = block & 1
        rel = ((block >> 3) - x) & 3
        upper = inner >= 128
        near = jnp.where(upper == (rel == 1), 512, jnp.where(rel == 1, 1152, 896))
        quarter = inner >> 6
        distant = jnp.where(quarter == 0, 1536, jnp.where(quarter == 3, 1408,
                            jnp.where(quarter == 2, 1664, 1792))) - p * 128
        base = jnp.where(rel == 0, 0, jnp.where(rel == 2, distant, near))
        column = jnp.where(((block >> 1) & 3) == y, base + p * 256 + inner, -1)
        fwd_pos[chunk * 128:(chunk + 1) * 128, 0:16] = jnp.transpose(column)

    def bwd_rows(index):
        block = index >> 8
        inner = index & 255
        rel = ((block & 3) - y) & 3
        upper = inner >= 128
        near = jnp.where(upper == (rel == 1), 256, jnp.where(rel == 1, 640, 384))
        quarter = inner >> 6
        distant = jnp.where(quarter == 0, 768, jnp.where(quarter == 3, 640,
                            jnp.where(quarter == 2, 768, 896)))
        base = jnp.where(rel == 0, 0, jnp.where(rel == 2, distant, near))
        hit = (block >> 2) == s * 4 + x
        return jnp.where(hit, base + inner, -1)

    def bwd_put(chunk, index):
        bwd_pos[:, chunk * 128:(chunk + 1) * 128] = bwd_rows(index)

    def bwd_half(rel, p, half):
        first = p * 256 + half * 128
        return bwd_raw[rel, :, first:first + 128]

    bwd_load.wait()
    for chunk in range(4):
        bwd_put(chunk, bwd_half(0, chunk // 2, chunk % 2))

    fwd_val[...] = jnp.zeros((1024, 128), F32)
    bwd_val[...] = jnp.zeros((16, 2048), F32)

    def pick_from(part, index, axis):
        return jnp.take_along_axis(part, index, axis=axis, mode="promise_in_bounds")

    def region(row, rows, col, cols):
        groups = range(row // 8, (row + rows) // 8)
        for tile in range(col, col + cols, 256):
            scores[row:row + rows, tile:tile + 256] = lax.dot_general(
                src_buf[row:row + rows, :], tgt_buf[tile:tile + 256, :],
                (((1,), (1,)), ((), ())), preferred_element_type=F32)
            chunks = (tile // 128, tile // 128 + 1)
            for chunk in chunks:
                at = slice(chunk * 128, chunk * 128 + 128)
                index0, index1 = bwd_pos[0:8, at], bwd_pos[8:16, at]
                pick0, pick1 = index0 & 7, index1 & 7
                where0, where1 = index0 >> 3, index1 >> 3
                value0, value1 = bwd_val[0:8, at], bwd_val[8:16, at]
                for group in groups:
                    part = scores[group * 8:group * 8 + 8, at]
                    value0 = jnp.where(where0 == group, pick_from(part, pick0, 0), value0)
                    value1 = jnp.where(where1 == group, pick_from(part, pick1, 0), value1)
                bwd_val[0:8, at] = value0
                bwd_val[8:16, at] = value1
            for group in groups:
                at = slice(group * 8, group * 8 + 8)
                index = fwd_pos[at, :]
                pick = index & 127
                where = index >> 7
                value = fwd_val[at, :]
                for chunk in chunks:
                    part = scores[at, chunk * 128:chunk * 128 + 128]
                    value = jnp.where(where == chunk, pick_from(part, pick, 1), value)
                fwd_val[at, :] = value

    region(0, 256, 0, 512)

    for copy in own_copies[:4]:
        copy.wait_recv()
    far_copies = (
        remote(srow(256, 64), srow(768, 64), 11, y_dev(1)),
        remote(srow(448, 64), srow(832, 64), 12, y_dev(3)),
        remote(trow(512 + c256, 64), trow(1536 + c128, 64), 13, x_dev(1)),
        remote(trow(704 + c256, 64), trow(1600 + c128, 64), 14, x_dev(3)),
        remote(srow(320, 64), srow(960, 64), 15, y_dev(1)),
        remote(srow(384, 64), srow(896, 64), 16, y_dev(3)),
        remote(trow(576 + c256, 64), trow(1856 + c128, 64), 17, x_dev(1)),
        remote(trow(640 + c256, 64), trow(1792 + c128, 64), 18, x_dev(3)),
    )
    for copy in far_copies:
        copy.start()
    partner = zc_dev(1)
    pass_copies = (
        remote(trow(512 + c256, 256), trow(512 + c256, 256), 19, partner),
        remote(trow(1024 + c256, 256), trow(1024 + c256, 256), 20, partner),
        remote(trow(1536 + c128, 128), trow(1536 + c128, 128), 21, partner),
        remote(trow(1792 + c128, 128), trow(1792 + c128, 128), 22, partner),
    )
    pass_copies[0].start()
    for copy in idx_copies:
        copy.wait_recv()
    for p in range(2):
        bwd_put(4 + 2 * p, bwd_half(3, p, 0))
        bwd_put(5 + 2 * p, bwd_half(1, p, 1))
        bwd_put(8 + 2 * p, bwd_half(3, p, 1))
        bwd_put(9 + 2 * p, bwd_half(1, p, 0))
        near, distant = far(bwd_half(2, p, 0), bwd_half(2, p, 1))
        bwd_put(12 + p, near)
        bwd_put(14 + p, distant)
    pass_copies[0].wait_recv()
    region(0, 256, 512, 512)
    region(256, 256, 0, 1024)

    for copy in own_copies[4:]:
        copy.wait_recv()
    pass_copies[1].start()
    region(512, 256, 0, 1024)
    pass_copies[1].wait_recv()
    region(0, 768, 1024, 512)

    for copy in far_copies[:4]:
        copy.wait_recv()
    pass_copies[2].start()
    region(768, 128, 0, 1536)
    pass_copies[2].wait_recv()
    region(0, 896, 1536, 256)

    for copy in far_copies[4:]:
        copy.wait_recv()
    pass_copies[3].start()
    region(896, 128, 0, 1792)
    pass_copies[3].wait_recv()
    region(0, 1024, 1792, 256)

    lane1 = lane[0:1, :]

    def bwd_sum(chunk):
        return jnp.sum(bwd_val[:, chunk * 128:(chunk + 1) * 128], axis=0, keepdims=True)

    def unfar(first, second):
        return jnp.where(lane1 < 64, first, second), jnp.where(lane1 < 64, second, first)

    def natural_cols(get):
        blocks = [[None] * 4 for _ in range(4)]
        for chunk in range(4):
            blocks[0][chunk] = get(chunk)
        for p in range(2):
            blocks[3][2 * p] = get(4 + 2 * p)
            blocks[1][2 * p + 1] = get(5 + 2 * p)
            blocks[3][2 * p + 1] = get(8 + 2 * p)
            blocks[1][2 * p] = get(9 + 2 * p)
            blocks[2][2 * p], blocks[2][2 * p + 1] = unfar(get(12 + p), get(14 + p))
        return blocks

    def natural_rows(get):
        blocks = [[None] * 2 for _ in range(4)]
        blocks[0] = [get(0), get(1)]
        blocks[3] = [get(2), get(4)]
        blocks[1] = [get(5), get(3)]
        blocks[2] = list(unfar(get(6), get(7)))
        return blocks

    for rel, rows in enumerate(natural_cols(bwd_sum)):
        for i, value in enumerate(rows):
            bwd_part[lax.rem(x + rel, 4), i:i + 1, :] = value
    bwd_z = [remote(bwd_part, bwd_zin.at[d - 1], 22 + d, zc_dev(d)) for d in range(1, 8)]
    for copy in bwd_z:
        copy.start()

    def fwd_sum(chunk):
        values = jnp.transpose(fwd_val[chunk * 128:(chunk + 1) * 128, :])
        return jnp.sum(values[0:16, :], axis=0, keepdims=True)

    for rel, rows in enumerate(natural_rows(fwd_sum)):
        for i, value in enumerate(rows):
            fwd_part[lax.rem(y + rel, 4), i:i + 1, :] = value
    fwd_y = [remote(fwd_part, fwd_in.at[d - 1], 29 + d, y_dev(d)) for d in range(1, 4)]
    for copy in fwd_y:
        copy.start()

    for copy in bwd_z:
        copy.wait_recv()
    total = bwd_part[...]
    for d in range(7):
        total = total + bwd_zin[d]
    bwd_two[...] = total
    bwd_x = [remote(bwd_two, bwd_xin.at[d - 1], 32 + d, x_dev(d)) for d in range(1, 4)]
    for copy in bwd_x:
        copy.start()

    for copy in fwd_y:
        copy.wait_recv()
    frow[...] = (fwd_part[...] + fwd_in[0] + fwd_in[1] + fwd_in[2]) * (1.0 / 16)

    def fwd_mean(rel, half):
        return frow[lax.rem(y + rel, 4), half:half + 1, :]

    m6, m7 = unfar(fwd_mean(2, 0), fwd_mean(2, 1))
    for chunk, row in enumerate((fwd_mean(0, 0), fwd_mean(0, 1), fwd_mean(3, 0), fwd_mean(1, 1),
                                 fwd_mean(3, 1), fwd_mean(1, 0), m6, m7)):
        fcol[chunk * 128:(chunk + 1) * 128, :] = jnp.transpose(jnp.broadcast_to(row, (128, 128)))

    for copy in bwd_x:
        copy.wait_recv()
    bwd_two2 = (bwd_two[...] + bwd_xin[0] + bwd_xin[1] + bwd_xin[2]) * (1.0 / 16)
    bwd_part2 = tgt_part
    bwd_part2[...] = bwd_two2

    def bwd_mean(rel, i):
        return bwd_part2[lax.rem(x + rel, 4), i:i + 1, :]

    def put_brow(chunk, value):
        brow[:, chunk * 128:(chunk + 1) * 128] = value

    for chunk in range(4):
        put_brow(chunk, bwd_mean(0, chunk))
    for p in range(2):
        put_brow(4 + 2 * p, bwd_mean(3, 2 * p))
        put_brow(5 + 2 * p, bwd_mean(1, 2 * p + 1))
        put_brow(8 + 2 * p, bwd_mean(3, 2 * p + 1))
        put_brow(9 + 2 * p, bwd_mean(1, 2 * p))
        near, distant = unfar(bwd_mean(2, 2 * p), bwd_mean(2, 2 * p + 1))
        put_brow(12 + p, near)
        put_brow(14 + p, distant)

    peaks = (jnp.zeros((8, 128), F32),) * 16
    for chunk_row in range(8):
        rel = ROW_REL[chunk_row]

        def margin_rows(g, peaks):
            at = pl.ds(aligned(chunk_row * 128 + g * 8, 8), 8)
            mean = fcol[at, :]
            best = jnp.zeros((8, 128), F32)
            new = []
            for chunk in range(16):
                cols = slice(chunk * 128, (chunk + 1) * 128)
                margin = (scores[at, cols] * weight[rel, :, cols]) / (mean + brow[:, cols])
                best = jnp.maximum(best, margin)
                new.append(jnp.maximum(peaks[chunk], margin))
            fwd_val[at, :] = best
            return tuple(new)

        peaks = lax.fori_loop(0, 16, margin_rows, peaks, unroll=2)

    def tgt_peak(chunk):
        return jnp.max(peaks[chunk], axis=0, keepdims=True)

    for rel, rows in enumerate(natural_cols(tgt_peak)):
        for i, value in enumerate(rows):
            tgt_part[lax.rem(x + rel, 4), i:i + 1, :] = value
    tgt_x = [remote(tgt_part.at[lax.rem(x + d, 4)], tgt_xin.at[d - 1], 35 + d, x_dev(d))
             for d in range(1, 4)]
    for copy in tgt_x:
        copy.start()

    def src_peak(chunk):
        values = jnp.transpose(fwd_val[chunk * 128:(chunk + 1) * 128, :])
        return jnp.max(values, axis=0, keepdims=True)

    for rel, rows in enumerate(natural_rows(src_peak)):
        for i, value in enumerate(rows):
            src_part[lax.rem(y + rel, 4), i:i + 1, :] = value
    src_y = [remote(src_part.at[lax.rem(y + d, 4)], src_in.at[d - 1], 38 + d, y_dev(d))
             for d in range(1, 4)]
    for copy in src_y:
        copy.start()

    for copy in tgt_x:
        copy.wait_recv()
    tgt_two[...] = jnp.maximum(jnp.maximum(tgt_part[x], tgt_xin[0]),
                               jnp.maximum(tgt_xin[1], tgt_xin[2]))
    tgt_z = [remote(tgt_two, tgt_zin.at[d - 1], 41 + d, zc_dev(d)) for d in range(1, 8)]
    for copy in tgt_z:
        copy.start()
    for copy in src_y:
        copy.wait_recv()
    src_out[...] = jnp.maximum(jnp.maximum(src_part[y], src_in[0]),
                               jnp.maximum(src_in[1], src_in[2]))
    for copy in tgt_z:
        copy.wait_recv()
    best = tgt_two[...]
    for d in range(7):
        best = jnp.maximum(best, tgt_zin[d])
    tgt_out[...] = best

    for copies in (own_copies, idx_copies, far_copies, pass_copies, bwd_z, fwd_y, bwd_x,
                   tgt_x, src_y, tgt_z):
        for copy in copies:
            copy.wait_send()


def body(src_emb, tgt_emb, pair_list, fwd_idx, bwd_idx):
    hbm = pl.BlockSpec(memory_space=pl.ANY)
    vmem = pl.BlockSpec(memory_space=pltpu.VMEM)
    src_best, tgt_best = pl.pallas_call(
        kernel,
        out_shape=(jax.ShapeDtypeStruct((2, 128), F32), jax.ShapeDtypeStruct((4, 128), F32)),
        in_specs=[hbm, hbm, pl.BlockSpec(memory_space=pltpu.SMEM), hbm, hbm],
        out_specs=(vmem, vmem),
        scratch_shapes=[
            pltpu.VMEM((256, D), BF16), pltpu.VMEM((512, D), BF16),
            pltpu.VMEM((1024, D), BF16), pltpu.VMEM((2048, D), BF16),
            pltpu.VMEM((1024, 2048), F32),
            pltpu.VMEM((16, 1024), I32), pltpu.VMEM((4, 16, 512), I32),
            pltpu.VMEM((1024, 128), I32), pltpu.VMEM((16, 2048), I32),
            pltpu.VMEM((1024, 128), F32), pltpu.VMEM((16, 2048), F32),
            pltpu.VMEM((4, 1, 2048), F32),
            pltpu.VMEM((4, 2, 128), F32), pltpu.VMEM((1024, 128), F32),
            pltpu.VMEM((1, 2048), F32),
            pltpu.VMEM((4, 2, 128), F32), pltpu.VMEM((3, 4, 2, 128), F32),
            pltpu.VMEM((4, 4, 128), F32), pltpu.VMEM((7, 4, 4, 128), F32),
            pltpu.VMEM((4, 4, 128), F32), pltpu.VMEM((3, 4, 4, 128), F32),
            pltpu.VMEM((4, 2, 128), F32), pltpu.VMEM((3, 2, 128), F32),
            pltpu.VMEM((4, 4, 128), F32), pltpu.VMEM((3, 4, 128), F32),
            pltpu.VMEM((4, 128), F32), pltpu.VMEM((7, 4, 128), F32),
            pltpu.SemaphoreType.DMA((4,)),
            pltpu.SemaphoreType.DMA((49,)), pltpu.SemaphoreType.DMA((49,)),
        ],
        compiler_params=pltpu.CompilerParams(
            collective_id=0, has_side_effects=True, vmem_limit_bytes=60 << 20),
    )(src_emb, tgt_emb, pair_list.T, fwd_idx.T, bwd_idx.T)
    return src_best.reshape(256), tgt_best.reshape(512)


def solution(mesh):
    return jax.shard_map(
        body,
        mesh=mesh,
        in_specs=(
            P(("src", "tgt"), None),
            P("tgt", None),
            P("src", None),
            P("src", None),
            P("tgt", None),
        ),
        out_specs=(P(("src", "tgt")), P("tgt")),
        check_vma=False,
    )
```

```python
import jax
import jax.numpy as jnp
from jax import lax
from jax.experimental import pallas as pl
from jax.experimental.pallas import tpu as pltpu
from jax.sharding import PartitionSpec as P

D = 1024
MESH = pl.DeviceIdType.MESH
F32 = jnp.float32
BF16 = jnp.bfloat16
I32 = jnp.int32

ROW_REL = (0, 0, 3, 1, 3, 1, 2, 2)
COL_SLOT = ((0, 0), (0, 0), (0, 1), (0, 1), (3, 0), (1, 0), (3, 1), (1, 1),
            (3, 0), (1, 0), (3, 1), (1, 1), (2, 0), (2, 1), (2, 0), (2, 1))


def aligned(value, step):
    return pl.multiple_of(value, step)


def kernel(src_hbm, tgt_hbm, pair_ref, fwd_hbm, bwd_hbm, src_out, tgt_out,
           src_raw, tgt_raw, src_buf, tgt_buf, scores, fwd_raw, bwd_raw, fwd_pos, bwd_pos,
           fwd_val, bwd_val, weight, frow, fcol, brow, fwd_part, fwd_in, bwd_part, bwd_zin,
           bwd_two, bwd_xin, src_part, src_in, tgt_part, tgt_xin, tgt_two, tgt_zin,
           load_sem, send_sem, recv_sem, ready_sem):
    s = lax.axis_index("src")
    t = lax.axis_index("tgt")
    core = lax.rem(s, 2)
    z = s // 2
    x = t // 4
    y = lax.rem(t, 4)

    def y_dev(d):
        return (s, 4 * x + lax.rem(y + d, 4))

    def x_dev(d):
        return (s, 4 * lax.rem(x + d, 4) + y)

    def zc_dev(d):
        dz, dc = d // 2, d % 2
        return (2 * lax.rem(z + dz, 4) + lax.rem(core + dc, 2), t)

    src_load = pltpu.make_async_copy(src_hbm, src_raw, load_sem.at[0])
    src_load.start()
    tgt_load = pltpu.make_async_copy(tgt_hbm, tgt_raw, load_sem.at[1])
    tgt_load.start()
    bwd_load = pltpu.make_async_copy(bwd_hbm, bwd_raw.at[0], load_sem.at[2])
    bwd_load.start()
    fwd_load = pltpu.make_async_copy(
        fwd_hbm.at[:, pl.ds(aligned(x * 1024, 1024), 1024)], fwd_raw, load_sem.at[3])
    fwd_load.start()

    barrier = pltpu.get_barrier_semaphore()
    for device in (y_dev(1), y_dev(3), x_dev(1), x_dev(3), zc_dev(1), zc_dev(2), zc_dev(6)):
        pl.semaphore_signal(barrier, inc=1, device_id=device, device_id_type=MESH)

    def remote(src, dst, sem, device):
        return pltpu.make_async_remote_copy(
            src_ref=src, dst_ref=dst, send_sem=send_sem.at[sem], recv_sem=recv_sem.at[sem],
            device_id=device, device_id_type=MESH)

    def normalise(raw, buf, raw_first, buf_first, count):
        def step(i, _):
            wide = raw[pl.ds(aligned(raw_first + i * 16, 16), 16), :].astype(F32)
            factor = lax.rsqrt(jnp.sum(wide * wide, axis=1, keepdims=True) + 1e-06)
            buf[pl.ds(aligned(buf_first + i * 16, 16), 16), :] = (wide * factor).astype(BF16)
            return 0
        lax.fori_loop(0, count // 16, step, 0, unroll=4)

    c256 = core * 256
    c128 = core * 128
    src_load.wait()
    normalise(src_raw, src_buf, 0, 0, 256)
    tgt_load.wait()
    normalise(tgt_raw, tgt_buf, c256, c256, 256)
    pl.semaphore_wait(barrier, 7)

    def srow(first, count):
        return src_buf.at[pl.ds(first, count), :]

    def trow(first, count, step=64):
        return tgt_buf.at[pl.ds(aligned(first, step), count), :]

    own_copies = (
        remote(srow(0, 128), srow(256, 128), 0, y_dev(1)),
        remote(srow(128, 128), srow(384, 128), 1, y_dev(3)),
        remote(trow(c256, 128), trow(512 + c256, 128), 2, x_dev(1)),
        remote(trow(c256 + 128, 128), trow(640 + c256, 128), 3, x_dev(3)),
        remote(srow(128, 128), srow(512, 128), 4, y_dev(1)),
        remote(srow(0, 128), srow(640, 128), 5, y_dev(3)),
        remote(trow(c256 + 128, 128), trow(1024 + c256, 128), 6, x_dev(1)),
        remote(trow(c256, 128), trow(1152 + c256, 128), 7, x_dev(3)),
    )
    idx_cols = pl.ds(aligned(c256, 256), 256)
    idx_copies = (
        remote(bwd_hbm.at[:, idx_cols], bwd_raw.at[3, :, idx_cols], 8, x_dev(1)),
        remote(bwd_hbm.at[:, idx_cols], bwd_raw.at[1, :, idx_cols], 9, x_dev(3)),
        remote(bwd_raw.at[3, :, idx_cols], bwd_raw.at[2, :, idx_cols], 10, x_dev(1)),
    )
    for copy in own_copies[:4]:
        copy.start()
    for copy in idx_copies[:2]:
        copy.start()
    for copy in own_copies[4:]:
        copy.start()
    for device in (zc_dev(2), zc_dev(6)):
        pl.semaphore_signal(ready_sem, inc=1, device_id=device, device_id_type=MESH)

    normalise(tgt_raw, tgt_buf, 256 - c256, 256 - c256, 256)

    def weight_row(rel, _):
        row = 4 * x + lax.rem(y + rel, 4)
        names = [pair_ref[k, row] for k in range(8)]
        for relx in range(4):
            for p in range(2):
                block = 2 * (4 * lax.rem(x + relx, 4) + y) + p
                hit = jnp.int32(0)
                for k in range(8):
                    hit = hit + jnp.where(names[k] == block, 1, 0)
                value = jnp.full((1, 128), jnp.where(hit > 0, 2.0, 0.0), F32)
                for chunk in range(16):
                    if COL_SLOT[chunk] == (relx, p):
                        weight[rel, :, chunk * 128:(chunk + 1) * 128] = value
        return 0

    lax.fori_loop(0, 4, weight_row, 0)

    lane = lax.broadcasted_iota(I32, (16, 128), 1)

    def far(first, second):
        return jnp.where(lane < 64, first, second), jnp.where(lane < 64, second, first)

    fwd_load.wait()
    fwd_pos[...] = jnp.full((1024, 128), -1, I32)

    def fwd_half(rel, half):
        return fwd_raw[:, pl.ds(aligned(lax.rem(y + rel, 4) * 256 + half * 128, 128), 128)]

    f6, f7 = far(fwd_half(2, 0), fwd_half(2, 1))
    fwd_chunks = (fwd_half(0, 0), fwd_half(0, 1), fwd_half(3, 0), fwd_half(1, 1),
                  fwd_half(3, 1), fwd_half(1, 0), f6, f7)
    for chunk, index in enumerate(fwd_chunks):
        block = index >> 8
        inner = index & 255
        p = block & 1
        rel = ((block >> 3) - x) & 3
        upper = inner >= 128
        near = jnp.where(upper == (rel == 1), 512, jnp.where(rel == 1, 1152, 896))
        quarter = inner >> 6
        distant = jnp.where(quarter == 0, 1536, jnp.where(quarter == 3, 1408,
                            jnp.where(quarter == 2, 1664, 1792))) - p * 128
        base = jnp.where(rel == 0, 0, jnp.where(rel == 2, distant, near))
        column = jnp.where(((block >> 1) & 3) == y, base + p * 256 + inner, -1)
        fwd_pos[chunk * 128:(chunk + 1) * 128, 0:16] = jnp.transpose(column)

    def bwd_rows(index):
        block = index >> 8
        inner = index & 255
        rel = ((block & 3) - y) & 3
        upper = inner >= 128
        near = jnp.where(upper == (rel == 1), 256, jnp.where(rel == 1, 640, 384))
        quarter = inner >> 6
        distant = jnp.where(quarter == 0, 768, jnp.where(quarter == 3, 640,
                            jnp.where(quarter == 2, 768, 896)))
        base = jnp.where(rel == 0, 0, jnp.where(rel == 2, distant, near))
        hit = (block >> 2) == s * 4 + x
        return jnp.where(hit, base + inner, -1)

    def bwd_put(chunk, index):
        bwd_pos[:, chunk * 128:(chunk + 1) * 128] = bwd_rows(index)

    def bwd_half(rel, p, half):
        first = p * 256 + half * 128
        return bwd_raw[rel, :, first:first + 128]

    bwd_load.wait()
    for chunk in range(4):
        bwd_put(chunk, bwd_half(0, chunk // 2, chunk % 2))

    fwd_val[...] = jnp.zeros((1024, 128), F32)
    bwd_val[...] = jnp.zeros((16, 2048), F32)

    def pick_from(part, index, axis):
        other = (1 - axis,)
        numbers = lax.GatherDimensionNumbers(
            offset_dims=(), collapsed_slice_dims=(axis,), start_index_map=(axis,),
            operand_batching_dims=other, start_indices_batching_dims=other)
        return lax.gather(part, index, numbers, (1, 1),
                          mode=lax.GatherScatterMode.PROMISE_IN_BOUNDS)

    def splat(value):
        return lax.full((8, 128), value, I32)

    def split(index, mask, shift):
        pick = lax.bitwise_and(index, splat(mask))
        return lax.expand_dims(pick, (2,)), lax.shift_right_arithmetic(index, splat(shift))

    def region(row, rows, col, cols):
        groups = range(row // 8, (row + rows) // 8)
        for tile in range(col, col + cols, 256):
            scores[row:row + rows, tile:tile + 256] = lax.dot_general(
                src_buf[row:row + rows, :], tgt_buf[tile:tile + 256, :],
                (((1,), (1,)), ((), ())), preferred_element_type=F32)
            chunks = (tile // 128, tile // 128 + 1)
            for chunk in chunks:
                at = slice(chunk * 128, chunk * 128 + 128)
                pick0, where0 = split(bwd_pos[0:8, at], 7, 3)
                pick1, where1 = split(bwd_pos[8:16, at], 7, 3)
                value0, value1 = bwd_val[0:8, at], bwd_val[8:16, at]
                for group in groups:
                    part = scores[group * 8:group * 8 + 8, at]
                    here = splat(group)
                    value0 = lax.select(lax.eq(where0, here), pick_from(part, pick0, 0), value0)
                    value1 = lax.select(lax.eq(where1, here), pick_from(part, pick1, 0), value1)
                bwd_val[0:8, at] = value0
                bwd_val[8:16, at] = value1
            for group in groups:
                at = slice(group * 8, group * 8 + 8)
                pick, where = split(fwd_pos[at, :], 127, 7)
                value = fwd_val[at, :]
                for chunk in chunks:
                    part = scores[at, chunk * 128:chunk * 128 + 128]
                    value = lax.select(lax.eq(where, splat(chunk)), pick_from(part, pick, 1), value)
                fwd_val[at, :] = value

    region(0, 256, 0, 512)

    for copy in own_copies[:4] + idx_copies[:2]:
        copy.wait_recv()
    idx_copies[2].start()
    far_copies = (
        remote(srow(256, 64), srow(768, 64), 11, y_dev(1)),
        remote(srow(448, 64), srow(832, 64), 12, y_dev(3)),
        remote(trow(512 + c256, 64), trow(1536 + c128, 64), 13, x_dev(1)),
        remote(trow(704 + c256, 64), trow(1600 + c128, 64), 14, x_dev(3)),
        remote(srow(320, 64), srow(960, 64), 15, y_dev(1)),
        remote(srow(384, 64), srow(896, 64), 16, y_dev(3)),
        remote(trow(576 + c256, 64), trow(1856 + c128, 64), 17, x_dev(1)),
        remote(trow(640 + c256, 64), trow(1792 + c128, 64), 18, x_dev(3)),
    )
    for copy in far_copies:
        copy.start()
    pl.semaphore_wait(ready_sem, 2)
    partner = zc_dev(1)

    def passed(first, count, sem):
        return remote(trow(first, count), trow(first, count), sem, partner)

    def passed_idx(rel, sem):
        piece = bwd_raw.at[rel, :, idx_cols]
        return remote(piece, piece, sem, partner)

    pass_copies = (
        passed(512 + c256, 256, 19), passed(1024 + c256, 256, 20),
        passed(1536 + c128, 64, 21), passed(1600 + c128, 64, 22),
        passed(1856 + c128, 64, 23), passed(1792 + c128, 64, 24),
        passed_idx(3, 25), passed_idx(1, 26), passed_idx(2, 27),
    )
    pass_copies[6].start()
    pass_copies[7].start()
    pass_copies[0].start()
    region(256, 256, 0, 512)
    pass_copies[6].wait_recv()
    pass_copies[7].wait_recv()
    for p in range(2):
        bwd_put(4 + 2 * p, bwd_half(3, p, 0))
        bwd_put(5 + 2 * p, bwd_half(1, p, 1))
        bwd_put(8 + 2 * p, bwd_half(3, p, 1))
        bwd_put(9 + 2 * p, bwd_half(1, p, 0))
    pass_copies[0].wait_recv()
    region(0, 512, 512, 512)

    for copy in own_copies[4:] + idx_copies[2:]:
        copy.wait_recv()
    pass_copies[1].start()
    pass_copies[8].start()
    region(512, 256, 0, 1024)
    pass_copies[1].wait_recv()
    pass_copies[8].wait_recv()
    for p in range(2):
        near, distant = far(bwd_half(2, p, 0), bwd_half(2, p, 1))
        bwd_put(12 + p, near)
        bwd_put(14 + p, distant)
    region(0, 768, 1024, 512)

    far_copies[2].wait_recv()
    pass_copies[2].start()
    far_copies[3].wait_recv()
    pass_copies[3].start()
    far_copies[0].wait_recv()
    far_copies[1].wait_recv()
    region(768, 128, 0, 1536)
    pass_copies[2].wait_recv()
    pass_copies[3].wait_recv()
    region(0, 896, 1536, 256)

    far_copies[6].wait_recv()
    pass_copies[4].start()
    far_copies[7].wait_recv()
    pass_copies[5].start()
    far_copies[4].wait_recv()
    far_copies[5].wait_recv()
    region(896, 128, 0, 1792)
    pass_copies[4].wait_recv()
    pass_copies[5].wait_recv()
    region(0, 1024, 1792, 256)

    lane1 = lane[0:1, :]

    def bwd_sum(chunk):
        return jnp.sum(bwd_val[:, chunk * 128:(chunk + 1) * 128], axis=0, keepdims=True)

    def unfar(first, second):
        if first is None:
            return None, None
        return jnp.where(lane1 < 64, first, second), jnp.where(lane1 < 64, second, first)

    def natural_cols(get):
        blocks = [[None] * 4 for _ in range(4)]
        for chunk in range(4):
            blocks[0][chunk] = get(chunk)
        for p in range(2):
            blocks[3][2 * p] = get(4 + 2 * p)
            blocks[1][2 * p + 1] = get(5 + 2 * p)
            blocks[3][2 * p + 1] = get(8 + 2 * p)
            blocks[1][2 * p] = get(9 + 2 * p)
            blocks[2][2 * p], blocks[2][2 * p + 1] = unfar(get(12 + p), get(14 + p))
        return blocks

    def natural_rows(get):
        blocks = [[None] * 2 for _ in range(4)]
        blocks[0] = [get(0), get(1)]
        blocks[3] = [get(2), get(4)]
        blocks[1] = [get(5), get(3)]
        blocks[2] = list(unfar(get(6), get(7)))
        return blocks

    for rel, rows in enumerate(natural_cols(bwd_sum)):
        for i, value in enumerate(rows):
            bwd_part[lax.rem(x + rel, 4), i:i + 1, :] = value
    bwd_z = [remote(bwd_part, bwd_zin.at[d - 1], 27 + d, zc_dev(d)) for d in range(1, 8)]
    for copy in bwd_z:
        copy.start()

    def fwd_sum(chunk):
        values = jnp.transpose(fwd_val[chunk * 128:(chunk + 1) * 128, :])
        return jnp.sum(values[0:16, :], axis=0, keepdims=True)

    for rel, rows in enumerate(natural_rows(fwd_sum)):
        for i, value in enumerate(rows):
            fwd_part[lax.rem(y + rel, 4), i:i + 1, :] = value
    fwd_y = [remote(fwd_part, fwd_in.at[d - 1], 34 + d, y_dev(d)) for d in range(1, 4)]
    for copy in fwd_y:
        copy.start()

    for copy in bwd_z:
        copy.wait_recv()
    total = bwd_part[...]
    for d in range(7):
        total = total + bwd_zin[d]
    bwd_two[...] = total
    bwd_x = [remote(bwd_two, bwd_xin.at[d - 1], 37 + d, x_dev(d)) for d in range(1, 4)]
    for copy in bwd_x:
        copy.start()

    for copy in fwd_y:
        copy.wait_recv()
    frow[...] = (fwd_part[...] + fwd_in[0] + fwd_in[1] + fwd_in[2]) * (1.0 / 16)

    def fwd_mean(rel, half):
        return frow[lax.rem(y + rel, 4), half:half + 1, :]

    m6, m7 = unfar(fwd_mean(2, 0), fwd_mean(2, 1))
    for chunk, row in enumerate((fwd_mean(0, 0), fwd_mean(0, 1), fwd_mean(3, 0), fwd_mean(1, 1),
                                 fwd_mean(3, 1), fwd_mean(1, 0), m6, m7)):
        fcol[chunk * 128:(chunk + 1) * 128, :] = jnp.transpose(jnp.broadcast_to(row, (128, 128)))

    for copy in bwd_x:
        copy.wait_recv()
    bwd_two2 = (bwd_two[...] + bwd_xin[0] + bwd_xin[1] + bwd_xin[2]) * (1.0 / 16)
    bwd_part2 = tgt_part
    bwd_part2[...] = bwd_two2

    def bwd_mean(rel, i):
        return bwd_part2[lax.rem(x + rel, 4), i:i + 1, :]

    def put_brow(chunk, value):
        brow[:, chunk * 128:(chunk + 1) * 128] = value

    for chunk in range(4):
        put_brow(chunk, bwd_mean(0, chunk))
    for p in range(2):
        put_brow(4 + 2 * p, bwd_mean(3, 2 * p))
        put_brow(5 + 2 * p, bwd_mean(1, 2 * p + 1))
        put_brow(8 + 2 * p, bwd_mean(3, 2 * p + 1))
        put_brow(9 + 2 * p, bwd_mean(1, 2 * p))
        near, distant = unfar(bwd_mean(2, 2 * p), bwd_mean(2, 2 * p + 1))
        put_brow(12 + p, near)
        put_brow(14 + p, distant)

    def margins(chunks, unroll, first):
        peaks = (jnp.zeros((8, 128), F32),) * len(chunks)
        for chunk_row in range(8):
            rel = ROW_REL[chunk_row]

            def margin_rows(g, peaks):
                at = pl.ds(aligned(chunk_row * 128 + g * 8, 8), 8)
                mean = fcol[at, :]
                best = jnp.zeros((8, 128), F32) if first else fwd_val[at, :]
                new = []
                for peak, chunk in zip(peaks, chunks):
                    cols = slice(chunk * 128, (chunk + 1) * 128)
                    margin = (scores[at, cols] * weight[rel, :, cols]) / (mean + brow[:, cols])
                    best = jnp.maximum(best, margin)
                    new.append(jnp.maximum(peak, margin))
                fwd_val[at, :] = best
                return tuple(new)

            peaks = lax.fori_loop(0, 16, margin_rows, peaks, unroll=unroll)
        return {chunk: jnp.max(peak, axis=0, keepdims=True) for chunk, peak in zip(chunks, peaks)}

    def put_peaks(peaks):
        for rel, rows in enumerate(natural_cols(peaks.get)):
            for i, value in enumerate(rows):
                if value is not None:
                    tgt_part[lax.rem(x + rel, 4), i:i + 1, :] = value

    put_peaks(margins(range(4, 16), 4, True))
    tgt_x = [remote(tgt_part.at[lax.rem(x + d, 4)], tgt_xin.at[d - 1], 40 + d, x_dev(d))
             for d in range(1, 4)]
    for copy in tgt_x:
        copy.start()
    own_peaks = margins(range(4), 8, False)
    for chunk, value in own_peaks.items():
        tgt_two[chunk:chunk + 1, :] = value

    def src_peak(chunk):
        values = jnp.transpose(fwd_val[chunk * 128:(chunk + 1) * 128, :])
        return jnp.max(values, axis=0, keepdims=True)

    for rel, rows in enumerate(natural_rows(src_peak)):
        for i, value in enumerate(rows):
            src_part[lax.rem(y + rel, 4), i:i + 1, :] = value
    src_y = [remote(src_part.at[lax.rem(y + d, 4)], src_in.at[d - 1], 43 + d, y_dev(d))
             for d in range(1, 4)]
    for copy in src_y:
        copy.start()

    for copy in tgt_x:
        copy.wait_recv()
    tgt_two[...] = jnp.maximum(jnp.maximum(tgt_two[...], tgt_xin[0]),
                               jnp.maximum(tgt_xin[1], tgt_xin[2]))
    tgt_z = [remote(tgt_two, tgt_zin.at[d - 1], 46 + d, zc_dev(d)) for d in range(1, 8)]
    for copy in tgt_z:
        copy.start()
    for copy in src_y:
        copy.wait_recv()
    src_out[...] = jnp.maximum(jnp.maximum(src_part[y], src_in[0]),
                               jnp.maximum(src_in[1], src_in[2]))
    for copy in tgt_z:
        copy.wait_recv()
    best = tgt_two[...]
    for d in range(7):
        best = jnp.maximum(best, tgt_zin[d])
    tgt_out[...] = best

    for copies in (own_copies, idx_copies, far_copies, pass_copies, bwd_z, fwd_y, bwd_x,
                   tgt_x, src_y, tgt_z):
        for copy in copies:
            copy.wait_send()


def body(src_emb, tgt_emb, pair_list, fwd_idx, bwd_idx):
    hbm = pl.BlockSpec(memory_space=pl.ANY)
    vmem = pl.BlockSpec(memory_space=pltpu.VMEM)
    src_best, tgt_best = pl.pallas_call(
        kernel,
        out_shape=(jax.ShapeDtypeStruct((2, 128), F32), jax.ShapeDtypeStruct((4, 128), F32)),
        in_specs=[hbm, hbm, pl.BlockSpec(memory_space=pltpu.SMEM), hbm, hbm],
        out_specs=(vmem, vmem),
        scratch_shapes=[
            pltpu.VMEM((256, D), BF16), pltpu.VMEM((512, D), BF16),
            pltpu.VMEM((1024, D), BF16), pltpu.VMEM((2048, D), BF16),
            pltpu.VMEM((1024, 2048), F32),
            pltpu.VMEM((16, 1024), I32), pltpu.VMEM((4, 16, 512), I32),
            pltpu.VMEM((1024, 128), I32), pltpu.VMEM((16, 2048), I32),
            pltpu.VMEM((1024, 128), F32), pltpu.VMEM((16, 2048), F32),
            pltpu.VMEM((4, 1, 2048), F32),
            pltpu.VMEM((4, 2, 128), F32), pltpu.VMEM((1024, 128), F32),
            pltpu.VMEM((1, 2048), F32),
            pltpu.VMEM((4, 2, 128), F32), pltpu.VMEM((3, 4, 2, 128), F32),
            pltpu.VMEM((4, 4, 128), F32), pltpu.VMEM((7, 4, 4, 128), F32),
            pltpu.VMEM((4, 4, 128), F32), pltpu.VMEM((3, 4, 4, 128), F32),
            pltpu.VMEM((4, 2, 128), F32), pltpu.VMEM((3, 2, 128), F32),
            pltpu.VMEM((4, 4, 128), F32), pltpu.VMEM((3, 4, 128), F32),
            pltpu.VMEM((4, 128), F32), pltpu.VMEM((7, 4, 128), F32),
            pltpu.SemaphoreType.DMA((4,)),
            pltpu.SemaphoreType.DMA((54,)), pltpu.SemaphoreType.DMA((54,)),
            pltpu.SemaphoreType.REGULAR,
        ],
        compiler_params=pltpu.CompilerParams(
            collective_id=0, has_side_effects=True, vmem_limit_bytes=60 << 20),
    )(src_emb, tgt_emb, pair_list.T, fwd_idx.T, bwd_idx.T)

    def flatten(src_ref, tgt_ref, src_flat, tgt_flat):
        src_flat[...] = src_ref[...].reshape(256)
        tgt_flat[...] = tgt_ref[...].reshape(512)

    return pl.pallas_call(
        flatten,
        out_shape=(jax.ShapeDtypeStruct((256,), F32), jax.ShapeDtypeStruct((512,), F32)),
        in_specs=[vmem, vmem],
        out_specs=(vmem, vmem),
    )(src_best, tgt_best)


def solution(mesh):
    return jax.shard_map(
        body,
        mesh=mesh,
        in_specs=(
            P(("src", "tgt"), None),
            P("tgt", None),
            P("src", None),
            P("src", None),
            P("tgt", None),
        ),
        out_specs=(P(("src", "tgt")), P("tgt")),
        check_vma=False,
    )
```

```python
import jax
import jax.numpy as jnp
from jax import lax
from jax.experimental import pallas as pl
from jax.experimental.pallas import tpu as pltpu
from jax.sharding import PartitionSpec as P

D = 1024
MESH = pl.DeviceIdType.MESH
F32 = jnp.float32
BF16 = jnp.bfloat16
I32 = jnp.int32

ROW_REL = (0, 0, 3, 1, 3, 1, 2, 2)
COL_SLOT = ((0, 0), (0, 0), (0, 1), (0, 1), (3, 0), (1, 0), (3, 1), (1, 1),
            (3, 0), (1, 0), (3, 1), (1, 1), (2, 0), (2, 1), (2, 0), (2, 1))


def aligned(value, step):
    return pl.multiple_of(value, step)


def kernel(src_hbm, tgt_hbm, pair_hbm, fwd_hbm, bwd_hbm, src_out, tgt_out, pair_ref,
           src_raw, tgt_raw, src_buf, tgt_buf, scores, fwd_raw, bwd_raw, fwd_pos, bwd_pos,
           fwd_val, bwd_val, weight, frow, fcol, brow, fwd_part, fwd_in, bwd_part, bwd_zin,
           bwd_two, bwd_xin, src_part, src_in, tgt_part, tgt_own, tgt_in, tgt_two, tgt_other,
           load_sem, send_sem, recv_sem, ready_sem):
    s = lax.axis_index("src")
    t = lax.axis_index("tgt")
    core = lax.rem(s, 2)
    z = s // 2
    x = t // 4
    y = lax.rem(t, 4)

    def y_dev(d):
        return (s, 4 * x + lax.rem(y + d, 4))

    def x_dev(d):
        return (s, 4 * lax.rem(x + d, 4) + y)

    def zc_dev(d):
        dz, dc = d // 2, d % 2
        return (2 * lax.rem(z + dz, 4) + lax.rem(core + dc, 2), t)

    src_load = pltpu.make_async_copy(src_hbm, src_raw, load_sem.at[0])
    src_load.start()
    tgt_load = pltpu.make_async_copy(tgt_hbm, tgt_raw, load_sem.at[1])
    tgt_load.start()
    bwd_load = pltpu.make_async_copy(bwd_hbm, bwd_raw.at[0], load_sem.at[2])
    bwd_load.start()
    fwd_load = pltpu.make_async_copy(
        fwd_hbm.at[:, pl.ds(aligned(x * 1024, 1024), 1024)], fwd_raw, load_sem.at[3])
    fwd_load.start()
    pair_load = pltpu.make_async_copy(pair_hbm, pair_ref, load_sem.at[4])
    pair_load.start()

    barrier = pltpu.get_barrier_semaphore()
    for device in (y_dev(1), y_dev(3), x_dev(1), x_dev(3), zc_dev(1), zc_dev(2), zc_dev(6)):
        pl.semaphore_signal(barrier, inc=1, device_id=device, device_id_type=MESH)

    def remote(src, dst, sem, device):
        return pltpu.make_async_remote_copy(
            src_ref=src, dst_ref=dst, send_sem=send_sem.at[sem], recv_sem=recv_sem.at[sem],
            device_id=device, device_id_type=MESH)

    def normalise(raw, buf, raw_first, buf_first, count):
        def step(i, _):
            wide = raw[pl.ds(aligned(raw_first + i * 16, 16), 16), :].astype(F32)
            factor = lax.rsqrt(jnp.sum(wide * wide, axis=1, keepdims=True) + 1e-06)
            buf[pl.ds(aligned(buf_first + i * 16, 16), 16), :] = (wide * factor).astype(BF16)
            return 0
        lax.fori_loop(0, count // 16, step, 0, unroll=4)

    c256 = core * 256
    c128 = core * 128
    src_load.wait()
    normalise(src_raw, src_buf, 0, 0, 256)
    tgt_load.wait()
    normalise(tgt_raw, tgt_buf, c256, c256, 256)
    pl.semaphore_wait(barrier, 7)

    def srow(first, count):
        return src_buf.at[pl.ds(first, count), :]

    def trow(first, count, step=64):
        return tgt_buf.at[pl.ds(aligned(first, step), count), :]

    own_copies = (
        remote(srow(0, 128), srow(256, 128), 0, y_dev(1)),
        remote(srow(128, 128), srow(384, 128), 1, y_dev(3)),
        remote(trow(c256, 128), trow(512 + c256, 128), 2, x_dev(1)),
        remote(trow(c256 + 128, 128), trow(640 + c256, 128), 3, x_dev(3)),
        remote(srow(128, 128), srow(512, 128), 4, y_dev(1)),
        remote(srow(0, 128), srow(640, 128), 5, y_dev(3)),
        remote(trow(c256 + 128, 128), trow(1024 + c256, 128), 6, x_dev(1)),
        remote(trow(c256, 128), trow(1152 + c256, 128), 7, x_dev(3)),
    )
    idx_cols = pl.ds(aligned(c256, 256), 256)
    idx_copies = (
        remote(bwd_hbm.at[:, idx_cols], bwd_raw.at[3, :, idx_cols], 8, x_dev(1)),
        remote(bwd_hbm.at[:, idx_cols], bwd_raw.at[1, :, idx_cols], 9, x_dev(3)),
        remote(bwd_raw.at[3, :, idx_cols], bwd_raw.at[2, :, idx_cols], 10, x_dev(1)),
    )
    for copy in own_copies[:4]:
        copy.start()
    for copy in idx_copies[:2]:
        copy.start()
    for copy in own_copies[4:]:
        copy.start()
    for device in (zc_dev(2), zc_dev(6)):
        pl.semaphore_signal(ready_sem, inc=1, device_id=device, device_id_type=MESH)

    normalise(tgt_raw, tgt_buf, 256 - c256, 256 - c256, 256)

    def weight_row(rel, _):
        row = 4 * x + lax.rem(y + rel, 4)
        names = [pair_ref[k, row] for k in range(8)]
        for relx in range(4):
            for p in range(2):
                block = 2 * (4 * lax.rem(x + relx, 4) + y) + p
                hit = jnp.int32(0)
                for k in range(8):
                    hit = hit + jnp.where(names[k] == block, 1, 0)
                value = jnp.full((1, 128), jnp.where(hit > 0, 2.0, 0.0), F32)
                for chunk in range(16):
                    if COL_SLOT[chunk] == (relx, p):
                        weight[rel, :, chunk * 128:(chunk + 1) * 128] = value
        return 0

    pair_load.wait()
    lax.fori_loop(0, 4, weight_row, 0)

    lane = lax.broadcasted_iota(I32, (16, 128), 1)

    def far(first, second):
        return jnp.where(lane < 64, first, second), jnp.where(lane < 64, second, first)

    fwd_load.wait()
    fwd_pos[...] = jnp.full((1024, 128), -1, I32)

    def fwd_half(rel, half):
        return fwd_raw[:, pl.ds(aligned(lax.rem(y + rel, 4) * 256 + half * 128, 128), 128)]

    f6, f7 = far(fwd_half(2, 0), fwd_half(2, 1))
    fwd_chunks = (fwd_half(0, 0), fwd_half(0, 1), fwd_half(3, 0), fwd_half(1, 1),
                  fwd_half(3, 1), fwd_half(1, 0), f6, f7)
    for chunk, index in enumerate(fwd_chunks):
        block = index >> 8
        inner = index & 255
        p = block & 1
        rel = ((block >> 3) - x) & 3
        upper = inner >= 128
        near = jnp.where(upper == (rel == 1), 512, jnp.where(rel == 1, 1152, 896))
        quarter = inner >> 6
        distant = jnp.where(quarter == 0, 1536, jnp.where(quarter == 3, 1408,
                            jnp.where(quarter == 2, 1664, 1792))) - p * 128
        base = jnp.where(rel == 0, 0, jnp.where(rel == 2, distant, near))
        column = jnp.where(((block >> 1) & 3) == y, base + p * 256 + inner, -1)
        fwd_pos[chunk * 128:(chunk + 1) * 128, 0:16] = jnp.transpose(column)

    def bwd_rows(index):
        block = index >> 8
        inner = index & 255
        rel = ((block & 3) - y) & 3
        upper = inner >= 128
        near = jnp.where(upper == (rel == 1), 256, jnp.where(rel == 1, 640, 384))
        quarter = inner >> 6
        distant = jnp.where(quarter == 0, 768, jnp.where(quarter == 3, 640,
                            jnp.where(quarter == 2, 768, 896)))
        base = jnp.where(rel == 0, 0, jnp.where(rel == 2, distant, near))
        hit = (block >> 2) == s * 4 + x
        return jnp.where(hit, base + inner, -1)

    def bwd_put(chunk, index):
        bwd_pos[:, chunk * 128:(chunk + 1) * 128] = bwd_rows(index)

    def bwd_half(rel, p, half):
        first = p * 256 + half * 128
        return bwd_raw[rel, :, first:first + 128]

    bwd_load.wait()
    for chunk in range(4):
        bwd_put(chunk, bwd_half(0, chunk // 2, chunk % 2))

    fwd_val[...] = jnp.zeros((1024, 128), F32)
    bwd_val[...] = jnp.zeros((16, 2048), F32)

    def pick_from(part, index, axis):
        other = (1 - axis,)
        numbers = lax.GatherDimensionNumbers(
            offset_dims=(), collapsed_slice_dims=(axis,), start_index_map=(axis,),
            operand_batching_dims=other, start_indices_batching_dims=other)
        return lax.gather(part, index, numbers, (1, 1),
                          mode=lax.GatherScatterMode.PROMISE_IN_BOUNDS)

    def splat(value):
        return lax.full((8, 128), value, I32)

    def split(index, mask, shift):
        pick = lax.bitwise_and(index, splat(mask))
        return lax.expand_dims(pick, (2,)), lax.shift_right_arithmetic(index, splat(shift))

    def region(row, rows, col, cols):
        groups = range(row // 8, (row + rows) // 8)
        for tile in range(col, col + cols, 256):
            scores[row:row + rows, tile:tile + 256] = lax.dot_general(
                src_buf[row:row + rows, :], tgt_buf[tile:tile + 256, :],
                (((1,), (1,)), ((), ())), preferred_element_type=F32)
            chunks = (tile // 128, tile // 128 + 1)
            for chunk in chunks:
                at = slice(chunk * 128, chunk * 128 + 128)
                pick0, where0 = split(bwd_pos[0:8, at], 7, 3)
                pick1, where1 = split(bwd_pos[8:16, at], 7, 3)
                value0, value1 = bwd_val[0:8, at], bwd_val[8:16, at]
                for group in groups:
                    part = scores[group * 8:group * 8 + 8, at]
                    here = splat(group)
                    value0 = lax.select(lax.eq(where0, here), pick_from(part, pick0, 0), value0)
                    value1 = lax.select(lax.eq(where1, here), pick_from(part, pick1, 0), value1)
                bwd_val[0:8, at] = value0
                bwd_val[8:16, at] = value1
            for group in groups:
                at = slice(group * 8, group * 8 + 8)
                pick, where = split(fwd_pos[at, :], 127, 7)
                value = fwd_val[at, :]
                for chunk in chunks:
                    part = scores[at, chunk * 128:chunk * 128 + 128]
                    value = lax.select(lax.eq(where, splat(chunk)), pick_from(part, pick, 1), value)
                fwd_val[at, :] = value

    region(0, 256, 0, 512)

    for copy in own_copies[:4] + idx_copies[:2]:
        copy.wait_recv()
    idx_copies[2].start()
    far_copies = (
        remote(srow(256, 64), srow(768, 64), 11, y_dev(1)),
        remote(srow(448, 64), srow(832, 64), 12, y_dev(3)),
        remote(trow(512 + c256, 64), trow(1536 + c128, 64), 13, x_dev(1)),
        remote(trow(704 + c256, 64), trow(1600 + c128, 64), 14, x_dev(3)),
        remote(srow(320, 64), srow(960, 64), 15, y_dev(1)),
        remote(srow(384, 64), srow(896, 64), 16, y_dev(3)),
        remote(trow(576 + c256, 64), trow(1856 + c128, 64), 17, x_dev(1)),
        remote(trow(640 + c256, 64), trow(1792 + c128, 64), 18, x_dev(3)),
    )
    for copy in far_copies:
        copy.start()
    pl.semaphore_wait(ready_sem, 2)
    partner = zc_dev(1)

    def passed(first, count, sem):
        return remote(trow(first, count), trow(first, count), sem, partner)

    def passed_idx(rel, sem):
        piece = bwd_raw.at[rel, :, idx_cols]
        return remote(piece, piece, sem, partner)

    pass_copies = (
        passed(512 + c256, 256, 19), passed(1024 + c256, 256, 20),
        passed(1536 + c128, 64, 21), passed(1600 + c128, 64, 22),
        passed(1856 + c128, 64, 23), passed(1792 + c128, 64, 24),
        passed_idx(3, 25), passed_idx(1, 26), passed_idx(2, 27),
    )
    pass_copies[6].start()
    pass_copies[7].start()
    pass_copies[0].start()
    region(256, 256, 0, 512)
    pass_copies[6].wait_recv()
    pass_copies[7].wait_recv()
    for p in range(2):
        bwd_put(4 + 2 * p, bwd_half(3, p, 0))
        bwd_put(5 + 2 * p, bwd_half(1, p, 1))
        bwd_put(8 + 2 * p, bwd_half(3, p, 1))
        bwd_put(9 + 2 * p, bwd_half(1, p, 0))
    pass_copies[0].wait_recv()
    region(0, 512, 512, 512)

    for copy in own_copies[4:] + idx_copies[2:]:
        copy.wait_recv()
    pass_copies[1].start()
    pass_copies[8].start()
    region(512, 256, 0, 1024)
    pass_copies[1].wait_recv()
    pass_copies[8].wait_recv()
    for p in range(2):
        near, distant = far(bwd_half(2, p, 0), bwd_half(2, p, 1))
        bwd_put(12 + p, near)
        bwd_put(14 + p, distant)
    region(0, 768, 1024, 512)

    far_copies[2].wait_recv()
    pass_copies[2].start()
    far_copies[3].wait_recv()
    pass_copies[3].start()
    far_copies[0].wait_recv()
    far_copies[1].wait_recv()
    region(768, 128, 0, 1536)
    pass_copies[2].wait_recv()
    pass_copies[3].wait_recv()
    region(0, 896, 1536, 256)

    far_copies[4].wait_recv()
    far_copies[5].wait_recv()
    region(896, 128, 0, 1024)
    far_copies[6].wait_recv()
    pass_copies[4].start()
    far_copies[7].wait_recv()
    pass_copies[5].start()
    region(896, 128, 1024, 768)
    pass_copies[4].wait_recv()
    pass_copies[5].wait_recv()
    region(0, 1024, 1792, 256)

    lane1 = lane[0:1, :]

    def bwd_sum(chunk):
        return jnp.sum(bwd_val[:, chunk * 128:(chunk + 1) * 128], axis=0, keepdims=True)

    def unfar(first, second):
        if first is None:
            return None, None
        return jnp.where(lane1 < 64, first, second), jnp.where(lane1 < 64, second, first)

    def natural_cols(get):
        blocks = [[None] * 4 for _ in range(4)]
        for chunk in range(4):
            blocks[0][chunk] = get(chunk)
        for p in range(2):
            blocks[3][2 * p] = get(4 + 2 * p)
            blocks[1][2 * p + 1] = get(5 + 2 * p)
            blocks[3][2 * p + 1] = get(8 + 2 * p)
            blocks[1][2 * p] = get(9 + 2 * p)
            blocks[2][2 * p], blocks[2][2 * p + 1] = unfar(get(12 + p), get(14 + p))
        return blocks

    def natural_rows(get):
        blocks = [[None] * 2 for _ in range(4)]
        blocks[0] = [get(0), get(1)]
        blocks[3] = [get(2), get(4)]
        blocks[1] = [get(5), get(3)]
        blocks[2] = list(unfar(get(6), get(7)))
        return blocks

    for rel, rows in enumerate(natural_cols(bwd_sum)):
        for i, value in enumerate(rows):
            bwd_part[lax.rem(x + rel, 4), i:i + 1, :] = value
    bwd_z = [remote(bwd_part, bwd_zin.at[d - 1], 27 + d, zc_dev(d)) for d in range(1, 8)]
    for copy in bwd_z:
        copy.start()

    def fwd_sum(chunk):
        values = jnp.transpose(fwd_val[chunk * 128:(chunk + 1) * 128, :])
        return jnp.sum(values[0:16, :], axis=0, keepdims=True)

    for rel, rows in enumerate(natural_rows(fwd_sum)):
        for i, value in enumerate(rows):
            fwd_part[lax.rem(y + rel, 4), i:i + 1, :] = value
    fwd_y = [remote(fwd_part, fwd_in.at[d - 1], 34 + d, y_dev(d)) for d in range(1, 4)]
    for copy in fwd_y:
        copy.start()

    for copy in bwd_z:
        copy.wait_recv()
    total = bwd_part[...]
    for d in range(7):
        total = total + bwd_zin[d]
    bwd_two[...] = total
    bwd_x = [remote(bwd_two, bwd_xin.at[d - 1], 37 + d, x_dev(d)) for d in range(1, 4)]
    for copy in bwd_x:
        copy.start()

    for copy in fwd_y:
        copy.wait_recv()
    frow[...] = (fwd_part[...] + fwd_in[0] + fwd_in[1] + fwd_in[2]) * (1.0 / 16)

    def fwd_mean(rel, half):
        return frow[lax.rem(y + rel, 4), half:half + 1, :]

    m6, m7 = unfar(fwd_mean(2, 0), fwd_mean(2, 1))
    for chunk, row in enumerate((fwd_mean(0, 0), fwd_mean(0, 1), fwd_mean(3, 0), fwd_mean(1, 1),
                                 fwd_mean(3, 1), fwd_mean(1, 0), m6, m7)):
        fcol[chunk * 128:(chunk + 1) * 128, :] = jnp.transpose(jnp.broadcast_to(row, (128, 128)))

    for copy in bwd_x:
        copy.wait_recv()
    bwd_two2 = (bwd_two[...] + bwd_xin[0] + bwd_xin[1] + bwd_xin[2]) * (1.0 / 16)
    bwd_part2 = tgt_part
    bwd_part2[...] = bwd_two2

    def bwd_mean(rel, i):
        return bwd_part2[lax.rem(x + rel, 4), i:i + 1, :]

    def put_brow(chunk, value):
        brow[:, chunk * 128:(chunk + 1) * 128] = value

    for chunk in range(4):
        put_brow(chunk, bwd_mean(0, chunk))
    for p in range(2):
        put_brow(4 + 2 * p, bwd_mean(3, 2 * p))
        put_brow(5 + 2 * p, bwd_mean(1, 2 * p + 1))
        put_brow(8 + 2 * p, bwd_mean(3, 2 * p + 1))
        put_brow(9 + 2 * p, bwd_mean(1, 2 * p))
        near, distant = unfar(bwd_mean(2, 2 * p), bwd_mean(2, 2 * p + 1))
        put_brow(12 + p, near)
        put_brow(14 + p, distant)

    def margins(chunks, unroll, first):
        peaks = (jnp.zeros((8, 128), F32),) * len(chunks)
        for chunk_row in range(8):
            rel = ROW_REL[chunk_row]

            def margin_rows(g, peaks):
                at = pl.ds(aligned(chunk_row * 128 + g * 8, 8), 8)
                mean = fcol[at, :]
                best = jnp.zeros((8, 128), F32) if first else fwd_val[at, :]
                new = []
                for peak, chunk in zip(peaks, chunks):
                    cols = slice(chunk * 128, (chunk + 1) * 128)
                    margin = (scores[at, cols] * weight[rel, :, cols]) / (mean + brow[:, cols])
                    best = jnp.maximum(best, margin)
                    new.append(jnp.maximum(peak, margin))
                fwd_val[at, :] = best
                return tuple(new)

            peaks = lax.fori_loop(0, 16, margin_rows, peaks, unroll=unroll)
        return {chunk: jnp.max(peak, axis=0, keepdims=True) for chunk, peak in zip(chunks, peaks)}

    def put_peaks(peaks):
        for rel, rows in enumerate(natural_cols(peaks.get)):
            for i, value in enumerate(rows):
                if value is not None:
                    tgt_part[lax.rem(x + rel, 4), i:i + 1, :] = value

    put_peaks(margins(range(4, 16), 4, True))
    def tgt_send(piece, dx, dz):
        device = (2 * lax.rem(z + dz, 4) + core, 4 * lax.rem(x + dx, 4) + y)
        place = 4 * dx + dz - 1
        return remote(piece, tgt_in.at[place], 41 + place, device)

    tgt_copies = [tgt_send(tgt_part.at[lax.rem(x + dx, 4)], dx, dz)
                  for dz in range(4) for dx in (2, 1, 3)]
    for copy in tgt_copies:
        copy.start()
    for chunk, value in margins(range(4), 8, False).items():
        tgt_own[chunk:chunk + 1, :] = value
    own_sends = [tgt_send(tgt_own, 0, dz) for dz in (2, 1, 3)]
    for copy in own_sends:
        copy.start()
    tgt_copies += own_sends

    def src_peak(chunk):
        values = jnp.transpose(fwd_val[chunk * 128:(chunk + 1) * 128, :])
        return jnp.max(values, axis=0, keepdims=True)

    for rel, rows in enumerate(natural_rows(src_peak)):
        for i, value in enumerate(rows):
            src_part[lax.rem(y + rel, 4), i:i + 1, :] = value
    src_y = [remote(src_part.at[lax.rem(y + d, 4)], src_in.at[d - 1], 56 + d, y_dev(d))
             for d in range(1, 4)]
    for copy in src_y:
        copy.start()

    for copy in tgt_copies:
        copy.wait_recv()
    best = tgt_own[...]
    for place in range(15):
        best = jnp.maximum(best, tgt_in[place])
    tgt_two[...] = best
    tgt_core = remote(tgt_two, tgt_other, 56, partner)
    tgt_core.start()
    for copy in src_y:
        copy.wait_recv()
    src_out[...] = jnp.maximum(jnp.maximum(src_part[y], src_in[0]),
                               jnp.maximum(src_in[1], src_in[2]))
    tgt_core.wait_recv()
    tgt_out[...] = jnp.maximum(best, tgt_other[...])

    for copies in (own_copies, idx_copies, far_copies, pass_copies, bwd_z, fwd_y, bwd_x,
                   tgt_copies, src_y, (tgt_core,)):
        for copy in copies:
            copy.wait_send()


def body(src_emb, tgt_emb, pair_list, fwd_idx, bwd_idx):
    hbm = pl.BlockSpec(memory_space=pl.ANY)
    vmem = pl.BlockSpec(memory_space=pltpu.VMEM)
    src_best, tgt_best = pl.pallas_call(
        kernel,
        out_shape=(jax.ShapeDtypeStruct((2, 128), F32), jax.ShapeDtypeStruct((4, 128), F32)),
        in_specs=[hbm] * 5,
        out_specs=(vmem, vmem),
        scratch_shapes=[
            pltpu.SMEM((8, 16), I32),
            pltpu.VMEM((256, D), BF16), pltpu.VMEM((512, D), BF16),
            pltpu.VMEM((1024, D), BF16), pltpu.VMEM((2048, D), BF16),
            pltpu.VMEM((1024, 2048), F32),
            pltpu.VMEM((16, 1024), I32), pltpu.VMEM((4, 16, 512), I32),
            pltpu.VMEM((1024, 128), I32), pltpu.VMEM((16, 2048), I32),
            pltpu.VMEM((1024, 128), F32), pltpu.VMEM((16, 2048), F32),
            pltpu.VMEM((4, 1, 2048), F32),
            pltpu.VMEM((4, 2, 128), F32), pltpu.VMEM((1024, 128), F32),
            pltpu.VMEM((1, 2048), F32),
            pltpu.VMEM((4, 2, 128), F32), pltpu.VMEM((3, 4, 2, 128), F32),
            pltpu.VMEM((4, 4, 128), F32), pltpu.VMEM((7, 4, 4, 128), F32),
            pltpu.VMEM((4, 4, 128), F32), pltpu.VMEM((3, 4, 4, 128), F32),
            pltpu.VMEM((4, 2, 128), F32), pltpu.VMEM((3, 2, 128), F32),
            pltpu.VMEM((4, 4, 128), F32), pltpu.VMEM((4, 128), F32),
            pltpu.VMEM((15, 4, 128), F32), pltpu.VMEM((4, 128), F32), pltpu.VMEM((4, 128), F32),
            pltpu.SemaphoreType.DMA((5,)),
            pltpu.SemaphoreType.DMA((60,)), pltpu.SemaphoreType.DMA((60,)),
            pltpu.SemaphoreType.REGULAR,
        ],
        compiler_params=pltpu.CompilerParams(
            collective_id=0, has_side_effects=True, vmem_limit_bytes=60 << 20),
    )(src_emb, tgt_emb, pair_list.T, fwd_idx.T, bwd_idx.T)

    def flatten(src_ref, tgt_ref, src_flat, tgt_flat):
        src_flat[...] = src_ref[...].reshape(256)
        tgt_flat[...] = tgt_ref[...].reshape(512)

    return pl.pallas_call(
        flatten,
        out_shape=(jax.ShapeDtypeStruct((256,), F32), jax.ShapeDtypeStruct((512,), F32)),
        in_specs=[vmem, vmem],
        out_specs=(vmem, vmem),
    )(src_best, tgt_best)


def solution(mesh):
    return jax.shard_map(
        body,
        mesh=mesh,
        in_specs=(
            P(("src", "tgt"), None),
            P("tgt", None),
            P("src", None),
            P("src", None),
            P("tgt", None),
        ),
        out_specs=(P(("src", "tgt")), P("tgt")),
        check_vma=False,
    )
```

```python
import jax
import jax.numpy as jnp
from jax import lax
from jax.experimental import pallas as pl
from jax.experimental.pallas import tpu as pltpu
from jax.sharding import PartitionSpec as P

D = 1024
MESH = pl.DeviceIdType.MESH
F32 = jnp.float32
BF16 = jnp.bfloat16
I32 = jnp.int32

COL_SLOT = ((0, 0), (0, 0), (0, 1), (0, 1), (3, 0), (1, 0), (3, 1), (1, 1),
            (3, 0), (1, 0), (3, 1), (1, 1), (2, 0), (2, 1), (2, 0), (2, 1))


def aligned(value, step):
    return pl.multiple_of(value, step)


def kernel(src_hbm, tgt_hbm, pair_hbm, fwd_hbm, bwd_hbm, src_out, tgt_out, pair_ref,
           src_raw, tgt_raw, src_buf, tgt_buf, scores, fwd_raw, bwd_raw, fwd_pos, bwd_pos,
           fwd_val, bwd_val, weight, frow, rowform, fcol, brow, fwd_part, fwd_in, bwd_part, bwd_zin,
           bwd_two, bwd_xin, src_part, src_in, tgt_part, tgt_own, tgt_in, tgt_two, tgt_other,
           load_sem, send_sem, recv_sem, ready_sem):
    s = lax.axis_index("src")
    t = lax.axis_index("tgt")
    core = lax.rem(s, 2)
    z = s // 2
    x = t // 4
    y = lax.rem(t, 4)

    def y_dev(d):
        return (s, 4 * x + lax.rem(y + d, 4))

    def x_dev(d):
        return (s, 4 * lax.rem(x + d, 4) + y)

    def zc_dev(d):
        dz, dc = d // 2, d % 2
        return (2 * lax.rem(z + dz, 4) + lax.rem(core + dc, 2), t)

    src_load = pltpu.make_async_copy(src_hbm, src_raw, load_sem.at[0])
    src_load.start()
    tgt_load = pltpu.make_async_copy(tgt_hbm, tgt_raw, load_sem.at[1])
    tgt_load.start()
    bwd_load = pltpu.make_async_copy(bwd_hbm, bwd_raw.at[0], load_sem.at[2])
    bwd_load.start()
    fwd_load = pltpu.make_async_copy(
        fwd_hbm.at[:, pl.ds(aligned(x * 1024, 1024), 1024)], fwd_raw, load_sem.at[3])
    fwd_load.start()
    pair_load = pltpu.make_async_copy(pair_hbm, pair_ref, load_sem.at[4])
    pair_load.start()

    barrier = pltpu.get_barrier_semaphore()
    for device in (y_dev(1), y_dev(3), x_dev(1), x_dev(3), zc_dev(1), zc_dev(2), zc_dev(6)):
        pl.semaphore_signal(barrier, inc=1, device_id=device, device_id_type=MESH)

    def remote(src, dst, sem, device):
        return pltpu.make_async_remote_copy(
            src_ref=src, dst_ref=dst, send_sem=send_sem.at[sem], recv_sem=recv_sem.at[sem],
            device_id=device, device_id_type=MESH)

    def normalise(raw, buf, raw_first, buf_first, count):
        def step(i, _):
            wide = raw[pl.ds(aligned(raw_first + i * 16, 16), 16), :].astype(F32)
            factor = lax.rsqrt(jnp.sum(wide * wide, axis=1, keepdims=True) + 1e-06)
            buf[pl.ds(aligned(buf_first + i * 16, 16), 16), :] = (wide * factor).astype(BF16)
            return 0
        lax.fori_loop(0, count // 16, step, 0, unroll=4)

    c256 = core * 256
    c128 = core * 128
    src_load.wait()
    normalise(src_raw, src_buf, 0, 0, 256)
    tgt_load.wait()
    normalise(tgt_raw, tgt_buf, c256, c256, 256)
    pl.semaphore_wait(barrier, 7)

    def srow(first, count):
        return src_buf.at[pl.ds(first, count), :]

    def trow(first, count, step=64):
        return tgt_buf.at[pl.ds(aligned(first, step), count), :]

    own_copies = (
        remote(srow(0, 128), srow(256, 128), 0, y_dev(1)),
        remote(srow(128, 128), srow(384, 128), 1, y_dev(3)),
        remote(trow(c256, 128), trow(512 + c256, 128), 2, x_dev(1)),
        remote(trow(c256 + 128, 128), trow(640 + c256, 128), 3, x_dev(3)),
        remote(srow(128, 128), srow(512, 128), 4, y_dev(1)),
        remote(srow(0, 128), srow(640, 128), 5, y_dev(3)),
        remote(trow(c256 + 128, 128), trow(1024 + c256, 128), 6, x_dev(1)),
        remote(trow(c256, 128), trow(1152 + c256, 128), 7, x_dev(3)),
    )
    idx_cols = pl.ds(aligned(c256, 256), 256)
    idx_copies = (
        remote(bwd_hbm.at[:, idx_cols], bwd_raw.at[3, :, idx_cols], 8, x_dev(1)),
        remote(bwd_hbm.at[:, idx_cols], bwd_raw.at[1, :, idx_cols], 9, x_dev(3)),
        remote(bwd_raw.at[3, :, idx_cols], bwd_raw.at[2, :, idx_cols], 10, x_dev(1)),
    )
    for copy in own_copies[:4]:
        copy.start()
    for copy in idx_copies[:2]:
        copy.start()
    for copy in own_copies[4:]:
        copy.start()
    for device in (zc_dev(2), zc_dev(6)):
        pl.semaphore_signal(ready_sem, inc=1, device_id=device, device_id_type=MESH)

    normalise(tgt_raw, tgt_buf, 256 - c256, 256 - c256, 256)

    def weight_row(kind, _):
        rel = lax.select(kind < 2, 0, lax.select(kind >= 6, 2, lax.select(kind % 2 == 0, 3, 1)))
        row = 4 * x + lax.rem(y + rel, 4)
        names = [pair_ref[k, row] for k in range(8)]
        for relx in range(4):
            for p in range(2):
                block = 2 * (4 * lax.rem(x + relx, 4) + y) + p
                hit = jnp.int32(0)
                for k in range(8):
                    hit = hit + jnp.where(names[k] == block, 1, 0)
                value = jnp.full((1, 128), jnp.where(hit > 0, 2.0, 0.0), F32)
                for chunk in range(16):
                    if COL_SLOT[chunk] == (relx, p):
                        weight[kind, :, chunk * 128:(chunk + 1) * 128] = value
        return 0

    pair_load.wait()
    lax.fori_loop(0, 8, weight_row, 0)

    lane = lax.broadcasted_iota(I32, (16, 128), 1)

    def far(first, second):
        return jnp.where(lane < 64, first, second), jnp.where(lane < 64, second, first)

    fwd_load.wait()
    fwd_pos[...] = jnp.full((1024, 128), -1, I32)

    def fwd_half(rel, half):
        return fwd_raw[:, pl.ds(aligned(lax.rem(y + rel, 4) * 256 + half * 128, 128), 128)]

    f6, f7 = far(fwd_half(2, 0), fwd_half(2, 1))
    fwd_chunks = (fwd_half(0, 0), fwd_half(0, 1), fwd_half(3, 0), fwd_half(1, 1),
                  fwd_half(3, 1), fwd_half(1, 0), f6, f7)
    for chunk, index in enumerate(fwd_chunks):
        block = index >> 8
        inner = index & 255
        p = block & 1
        rel = ((block >> 3) - x) & 3
        upper = inner >= 128
        near = jnp.where(upper == (rel == 1), 512, jnp.where(rel == 1, 1152, 896))
        quarter = inner >> 6
        distant = jnp.where(quarter == 0, 1536, jnp.where(quarter == 3, 1408,
                            jnp.where(quarter == 2, 1664, 1792))) - p * 128
        base = jnp.where(rel == 0, 0, jnp.where(rel == 2, distant, near))
        column = jnp.where(((block >> 1) & 3) == y, base + p * 256 + inner, -1)
        fwd_pos[chunk * 128:(chunk + 1) * 128, 0:16] = jnp.transpose(column)

    def bwd_rows(index):
        block = index >> 8
        inner = index & 255
        rel = ((block & 3) - y) & 3
        upper = inner >= 128
        near = jnp.where(upper == (rel == 1), 256, jnp.where(rel == 1, 640, 384))
        quarter = inner >> 6
        distant = jnp.where(quarter == 0, 768, jnp.where(quarter == 3, 640,
                            jnp.where(quarter == 2, 768, 896)))
        base = jnp.where(rel == 0, 0, jnp.where(rel == 2, distant, near))
        hit = (block >> 2) == s * 4 + x
        return jnp.where(hit, base + inner, -1)

    def bwd_put(chunk, index):
        bwd_pos[:, chunk * 128:(chunk + 1) * 128] = bwd_rows(index)

    def bwd_half(rel, p, half):
        first = p * 256 + half * 128
        return bwd_raw[rel, :, first:first + 128]

    bwd_load.wait()
    for chunk in range(4):
        bwd_put(chunk, bwd_half(0, chunk // 2, chunk % 2))

    fwd_val[...] = jnp.zeros((1024, 128), F32)
    bwd_val[...] = jnp.zeros((16, 2048), F32)

    def pick_from(part, index, axis):
        other = (1 - axis,)
        numbers = lax.GatherDimensionNumbers(
            offset_dims=(), collapsed_slice_dims=(axis,), start_index_map=(axis,),
            operand_batching_dims=other, start_indices_batching_dims=other)
        return lax.gather(part, index, numbers, (1, 1),
                          mode=lax.GatherScatterMode.PROMISE_IN_BOUNDS)

    def splat(value):
        return lax.full((8, 128), value, I32)

    def split(index, mask, shift):
        pick = lax.bitwise_and(index, splat(mask))
        return lax.expand_dims(pick, (2,)), lax.shift_right_arithmetic(index, splat(shift))

    def region(row, rows, col, cols):
        groups = range(row // 8, (row + rows) // 8)
        for tile in range(col, col + cols, 256):
            scores[row:row + rows, tile:tile + 256] = lax.dot_general(
                src_buf[row:row + rows, :], tgt_buf[tile:tile + 256, :],
                (((1,), (1,)), ((), ())), preferred_element_type=F32)
            chunks = (tile // 128, tile // 128 + 1)
            for chunk in chunks:
                at = slice(chunk * 128, chunk * 128 + 128)
                pick0, where0 = split(bwd_pos[0:8, at], 7, 3)
                pick1, where1 = split(bwd_pos[8:16, at], 7, 3)
                value0, value1 = bwd_val[0:8, at], bwd_val[8:16, at]
                for group in groups:
                    part = scores[group * 8:group * 8 + 8, at]
                    here = splat(group)
                    value0 = lax.select(lax.eq(where0, here), pick_from(part, pick0, 0), value0)
                    value1 = lax.select(lax.eq(where1, here), pick_from(part, pick1, 0), value1)
                bwd_val[0:8, at] = value0
                bwd_val[8:16, at] = value1
            for group in groups:
                at = slice(group * 8, group * 8 + 8)
                pick, where = split(fwd_pos[at, :], 127, 7)
                value = fwd_val[at, :]
                for chunk in chunks:
                    part = scores[at, chunk * 128:chunk * 128 + 128]
                    value = lax.select(lax.eq(where, splat(chunk)), pick_from(part, pick, 1), value)
                fwd_val[at, :] = value

    region(0, 256, 0, 512)

    for copy in own_copies[:4] + idx_copies[:2]:
        copy.wait_recv()
    idx_copies[2].start()
    far_copies = (
        remote(srow(256, 64), srow(768, 64), 11, y_dev(1)),
        remote(srow(448, 64), srow(832, 64), 12, y_dev(3)),
        remote(trow(512 + c256, 64), trow(1536 + c128, 64), 13, x_dev(1)),
        remote(trow(704 + c256, 64), trow(1600 + c128, 64), 14, x_dev(3)),
        remote(srow(320, 64), srow(960, 64), 15, y_dev(1)),
        remote(srow(384, 64), srow(896, 64), 16, y_dev(3)),
        remote(trow(576 + c256, 64), trow(1856 + c128, 64), 17, x_dev(1)),
        remote(trow(640 + c256, 64), trow(1792 + c128, 64), 18, x_dev(3)),
    )
    for copy in far_copies:
        copy.start()
    pl.semaphore_wait(ready_sem, 2)
    partner = zc_dev(1)

    def passed(first, count, sem):
        return remote(trow(first, count), trow(first, count), sem, partner)

    def passed_idx(rel, sem):
        piece = bwd_raw.at[rel, :, idx_cols]
        return remote(piece, piece, sem, partner)

    pass_copies = (
        passed(512 + c256, 256, 19), passed(1024 + c256, 256, 20),
        passed(1536 + c128, 64, 21), passed(1600 + c128, 64, 22),
        passed(1856 + c128, 64, 23), passed(1792 + c128, 64, 24),
        passed_idx(3, 25), passed_idx(1, 26), passed_idx(2, 27),
    )
    pass_copies[6].start()
    pass_copies[7].start()
    pass_copies[0].start()
    region(256, 256, 0, 512)
    pass_copies[6].wait_recv()
    pass_copies[7].wait_recv()
    for p in range(2):
        bwd_put(4 + 2 * p, bwd_half(3, p, 0))
        bwd_put(5 + 2 * p, bwd_half(1, p, 1))
        bwd_put(8 + 2 * p, bwd_half(3, p, 1))
        bwd_put(9 + 2 * p, bwd_half(1, p, 0))
    pass_copies[0].wait_recv()
    region(0, 512, 512, 512)

    for copy in own_copies[4:] + idx_copies[2:]:
        copy.wait_recv()
    pass_copies[1].start()
    pass_copies[8].start()
    region(512, 256, 0, 1024)
    pass_copies[1].wait_recv()
    pass_copies[8].wait_recv()
    for p in range(2):
        near, distant = far(bwd_half(2, p, 0), bwd_half(2, p, 1))
        bwd_put(12 + p, near)
        bwd_put(14 + p, distant)
    region(0, 768, 1024, 512)

    far_copies[2].wait_recv()
    pass_copies[2].start()
    far_copies[3].wait_recv()
    pass_copies[3].start()
    pass_copies[2].wait_recv()
    pass_copies[3].wait_recv()
    region(0, 768, 1536, 256)

    for copy in far_copies[:2] + far_copies[4:6]:
        copy.wait_recv()
    region(768, 256, 0, 768)
    far_copies[6].wait_recv()
    pass_copies[4].start()
    far_copies[7].wait_recv()
    pass_copies[5].start()
    region(768, 256, 768, 1024)
    pass_copies[4].wait_recv()
    pass_copies[5].wait_recv()
    region(0, 1024, 1792, 256)

    lane1 = lane[0:1, :]

    def bwd_sum(chunk):
        return jnp.sum(bwd_val[:, chunk * 128:(chunk + 1) * 128], axis=0, keepdims=True)

    def unfar(first, second):
        if first is None:
            return None, None
        return jnp.where(lane1 < 64, first, second), jnp.where(lane1 < 64, second, first)

    def natural_cols(get):
        blocks = [[None] * 4 for _ in range(4)]
        for chunk in range(4):
            blocks[0][chunk] = get(chunk)
        for p in range(2):
            blocks[3][2 * p] = get(4 + 2 * p)
            blocks[1][2 * p + 1] = get(5 + 2 * p)
            blocks[3][2 * p + 1] = get(8 + 2 * p)
            blocks[1][2 * p] = get(9 + 2 * p)
            blocks[2][2 * p], blocks[2][2 * p + 1] = unfar(get(12 + p), get(14 + p))
        return blocks

    def natural_rows(get):
        blocks = [[None] * 2 for _ in range(4)]
        blocks[0] = [get(0), get(1)]
        blocks[3] = [get(2), get(4)]
        blocks[1] = [get(5), get(3)]
        blocks[2] = list(unfar(get(6), get(7)))
        return blocks

    for rel, rows in enumerate(natural_cols(bwd_sum)):
        for i, value in enumerate(rows):
            bwd_part[lax.rem(x + rel, 4), i:i + 1, :] = value
    bwd_z = [remote(bwd_part, bwd_zin.at[d - 1], 27 + d, zc_dev(d)) for d in range(1, 8)]
    for copy in bwd_z:
        copy.start()

    def to_rows(combine):
        def step(chunk, _):
            at = pl.ds(aligned(chunk * 128, 128), 128)
            rowform[chunk] = combine(jnp.transpose(fwd_val[at, :]))
            return 0
        lax.fori_loop(0, 8, step, 0)

    def row_of(chunk):
        return rowform[chunk]

    to_rows(lambda values: jnp.sum(values[0:16, :], axis=0, keepdims=True))
    for rel, rows in enumerate(natural_rows(row_of)):
        for i, value in enumerate(rows):
            fwd_part[lax.rem(y + rel, 4), i:i + 1, :] = value
    fwd_y = [remote(fwd_part, fwd_in.at[d - 1], 34 + d, y_dev(d)) for d in range(1, 4)]
    for copy in fwd_y:
        copy.start()

    for copy in bwd_z:
        copy.wait_recv()
    total = bwd_part[...]
    for d in range(7):
        total = total + bwd_zin[d]
    bwd_two[...] = total
    bwd_x = [remote(bwd_two, bwd_xin.at[d - 1], 37 + d, x_dev(d)) for d in range(1, 4)]
    for copy in bwd_x:
        copy.start()

    for copy in fwd_y:
        copy.wait_recv()
    frow[...] = (fwd_part[...] + fwd_in[0] + fwd_in[1] + fwd_in[2]) * (1.0 / 16)

    def fwd_mean(rel, half):
        return frow[lax.rem(y + rel, 4), half:half + 1, :]

    m6, m7 = unfar(fwd_mean(2, 0), fwd_mean(2, 1))
    for chunk, row in enumerate((fwd_mean(0, 0), fwd_mean(0, 1), fwd_mean(3, 0), fwd_mean(1, 1),
                                 fwd_mean(3, 1), fwd_mean(1, 0), m6, m7)):
        rowform[chunk] = row

    def spread(chunk, _):
        at = pl.ds(aligned(chunk * 128, 128), 128)
        fcol[at, :] = jnp.transpose(jnp.broadcast_to(rowform[chunk], (128, 128)))
        return 0

    lax.fori_loop(0, 8, spread, 0)

    for copy in bwd_x:
        copy.wait_recv()
    bwd_two2 = (bwd_two[...] + bwd_xin[0] + bwd_xin[1] + bwd_xin[2]) * (1.0 / 16)
    bwd_part2 = tgt_part
    bwd_part2[...] = bwd_two2

    def bwd_mean(rel, i):
        return bwd_part2[lax.rem(x + rel, 4), i:i + 1, :]

    def put_brow(chunk, value):
        brow[:, chunk * 128:(chunk + 1) * 128] = value

    for chunk in range(4):
        put_brow(chunk, bwd_mean(0, chunk))
    for p in range(2):
        put_brow(4 + 2 * p, bwd_mean(3, 2 * p))
        put_brow(5 + 2 * p, bwd_mean(1, 2 * p + 1))
        put_brow(8 + 2 * p, bwd_mean(3, 2 * p + 1))
        put_brow(9 + 2 * p, bwd_mean(1, 2 * p))
        near, distant = unfar(bwd_mean(2, 2 * p), bwd_mean(2, 2 * p + 1))
        put_brow(12 + p, near)
        put_brow(14 + p, distant)

    def margins(chunks, unroll, first):
        def margin_rows(step, peaks):
            peaks = list(peaks)
            kind = step // (16 // unroll)
            for g in range(unroll):
                at = pl.ds(aligned(step * (8 * unroll) + g * 8, 8), 8)
                mean = fcol[at, :]
                best = jnp.zeros((8, 128), F32) if first else fwd_val[at, :]
                for i, chunk in enumerate(chunks):
                    cols = slice(chunk * 128, (chunk + 1) * 128)
                    margin = (scores[at, cols] * weight[kind, :, cols]) / (mean + brow[:, cols])
                    best = jnp.maximum(best, margin)
                    peaks[i] = jnp.maximum(peaks[i], margin)
                fwd_val[at, :] = best
            return tuple(peaks)

        peaks = lax.fori_loop(0, 128 // unroll, margin_rows,
                              (jnp.zeros((8, 128), F32),) * len(chunks))
        return {chunk: jnp.max(peak, axis=0, keepdims=True) for chunk, peak in zip(chunks, peaks)}

    def put_peaks(peaks):
        for rel, rows in enumerate(natural_cols(peaks.get)):
            for i, value in enumerate(rows):
                if value is not None:
                    tgt_part[lax.rem(x + rel, 4), i:i + 1, :] = value

    put_peaks(margins(range(4, 16), 4, True))
    def tgt_send(piece, dx, dz):
        device = (2 * lax.rem(z + dz, 4) + core, 4 * lax.rem(x + dx, 4) + y)
        place = 4 * dx + dz - 1
        return remote(piece, tgt_in.at[place], 41 + place, device)

    tgt_copies = [tgt_send(tgt_part.at[lax.rem(x + dx, 4)], dx, dz)
                  for dz in range(4) for dx in (2, 1, 3)]
    for copy in tgt_copies:
        copy.start()
    for chunk, value in margins(range(4), 8, False).items():
        tgt_own[chunk:chunk + 1, :] = value
    own_sends = [tgt_send(tgt_own, 0, dz) for dz in (2, 1, 3)]
    for copy in own_sends:
        copy.start()
    tgt_copies += own_sends

    to_rows(lambda values: jnp.max(values, axis=0, keepdims=True))
    for rel, rows in enumerate(natural_rows(row_of)):
        for i, value in enumerate(rows):
            src_part[lax.rem(y + rel, 4), i:i + 1, :] = value
    src_y = [remote(src_part.at[lax.rem(y + d, 4)], src_in.at[d - 1], 56 + d, y_dev(d))
             for d in range(1, 4)]
    for copy in src_y:
        copy.start()

    for copy in tgt_copies:
        copy.wait_recv()
    best = tgt_own[...]
    for place in range(15):
        best = jnp.maximum(best, tgt_in[place])
    tgt_two[...] = best
    tgt_core = remote(tgt_two, tgt_other, 56, partner)
    tgt_core.start()
    for copy in src_y:
        copy.wait_recv()
    src_out[...] = jnp.maximum(jnp.maximum(src_part[y], src_in[0]),
                               jnp.maximum(src_in[1], src_in[2]))
    tgt_core.wait_recv()
    tgt_out[...] = jnp.maximum(best, tgt_other[...])

    for copies in (own_copies, idx_copies, far_copies, pass_copies, bwd_z, fwd_y, bwd_x,
                   tgt_copies, src_y, (tgt_core,)):
        for copy in copies:
            copy.wait_send()


def body(src_emb, tgt_emb, pair_list, fwd_idx, bwd_idx):
    hbm = pl.BlockSpec(memory_space=pl.ANY)
    vmem = pl.BlockSpec(memory_space=pltpu.VMEM)
    src_best, tgt_best = pl.pallas_call(
        kernel,
        out_shape=(jax.ShapeDtypeStruct((2, 128), F32), jax.ShapeDtypeStruct((4, 128), F32)),
        in_specs=[hbm] * 5,
        out_specs=(vmem, vmem),
        scratch_shapes=[
            pltpu.SMEM((8, 16), I32),
            pltpu.VMEM((256, D), BF16), pltpu.VMEM((512, D), BF16),
            pltpu.VMEM((1024, D), BF16), pltpu.VMEM((2048, D), BF16),
            pltpu.VMEM((1024, 2048), F32),
            pltpu.VMEM((16, 1024), I32), pltpu.VMEM((4, 16, 512), I32),
            pltpu.VMEM((1024, 128), I32), pltpu.VMEM((16, 2048), I32),
            pltpu.VMEM((1024, 128), F32), pltpu.VMEM((16, 2048), F32),
            pltpu.VMEM((8, 1, 2048), F32),
            pltpu.VMEM((4, 2, 128), F32), pltpu.VMEM((8, 1, 128), F32), pltpu.VMEM((1024, 128), F32),
            pltpu.VMEM((1, 2048), F32),
            pltpu.VMEM((4, 2, 128), F32), pltpu.VMEM((3, 4, 2, 128), F32),
            pltpu.VMEM((4, 4, 128), F32), pltpu.VMEM((7, 4, 4, 128), F32),
            pltpu.VMEM((4, 4, 128), F32), pltpu.VMEM((3, 4, 4, 128), F32),
            pltpu.VMEM((4, 2, 128), F32), pltpu.VMEM((3, 2, 128), F32),
            pltpu.VMEM((4, 4, 128), F32), pltpu.VMEM((4, 128), F32),
            pltpu.VMEM((15, 4, 128), F32), pltpu.VMEM((4, 128), F32), pltpu.VMEM((4, 128), F32),
            pltpu.SemaphoreType.DMA((5,)),
            pltpu.SemaphoreType.DMA((60,)), pltpu.SemaphoreType.DMA((60,)),
            pltpu.SemaphoreType.REGULAR,
        ],
        compiler_params=pltpu.CompilerParams(
            collective_id=0, has_side_effects=True, vmem_limit_bytes=60 << 20),
    )(src_emb, tgt_emb, pair_list.T, fwd_idx.T, bwd_idx.T)

    def flatten(src_ref, tgt_ref, src_flat, tgt_flat):
        src_flat[...] = src_ref[...].reshape(256)
        tgt_flat[...] = tgt_ref[...].reshape(512)

    return pl.pallas_call(
        flatten,
        out_shape=(jax.ShapeDtypeStruct((256,), F32), jax.ShapeDtypeStruct((512,), F32)),
        in_specs=[vmem, vmem],
        out_specs=(vmem, vmem),
    )(src_best, tgt_best)


def solution(mesh):
    return jax.shard_map(
        body,
        mesh=mesh,
        in_specs=(
            P(("src", "tgt"), None),
            P("tgt", None),
            P("src", None),
            P("src", None),
            P("tgt", None),
        ),
        out_specs=(P(("src", "tgt")), P("tgt")),
        check_vma=False,
    )
```

```python
import jax
import jax.numpy as jnp
from jax import lax
from jax.experimental import pallas as pl
from jax.experimental.pallas import tpu as pltpu
from jax.sharding import PartitionSpec as P

D = 1024
MESH = pl.DeviceIdType.MESH
F32 = jnp.float32
BF16 = jnp.bfloat16
I32 = jnp.int32

COL_SLOT = ((0, 0), (0, 0), (0, 1), (0, 1), (3, 0), (1, 0), (3, 1), (1, 1),
            (3, 0), (1, 0), (3, 1), (1, 1), (2, 0), (2, 1), (2, 0), (2, 1))


def aligned(value, step):
    return pl.multiple_of(value, step)


def kernel(src_hbm, tgt_hbm, pair_hbm, fwd_hbm, bwd_hbm, src_out, tgt_out, pair_ref,
           src_raw, tgt_raw, src_buf, tgt_buf, scores, fwd_raw, bwd_raw, fwd_pos, bwd_pos,
           fwd_val, bwd_val, weight, frow, rowform, fcol, brow, fwd_part, fwd_in, bwd_part, bwd_zin,
           bwd_two, bwd_xin, src_part, src_in, tgt_part, tgt_own, tgt_in, tgt_two, tgt_other,
           load_sem, send_sem, recv_sem, ready_sem):
    s = lax.axis_index("src")
    t = lax.axis_index("tgt")
    core = lax.rem(s, 2)
    z = s // 2
    x = t // 4
    y = lax.rem(t, 4)

    def y_dev(d):
        return (s, 4 * x + lax.rem(y + d, 4))

    def x_dev(d):
        return (s, 4 * lax.rem(x + d, 4) + y)

    def zc_dev(d):
        dz, dc = d // 2, d % 2
        return (2 * lax.rem(z + dz, 4) + lax.rem(core + dc, 2), t)

    src_load = pltpu.make_async_copy(src_hbm, src_raw, load_sem.at[0])
    src_load.start()
    tgt_load = pltpu.make_async_copy(tgt_hbm, tgt_raw, load_sem.at[1])
    tgt_load.start()
    bwd_load = pltpu.make_async_copy(bwd_hbm, bwd_raw.at[0], load_sem.at[2])
    bwd_load.start()
    fwd_load = pltpu.make_async_copy(
        fwd_hbm.at[:, pl.ds(aligned(x * 1024, 1024), 1024)], fwd_raw, load_sem.at[3])
    fwd_load.start()
    pair_load = pltpu.make_async_copy(pair_hbm, pair_ref, load_sem.at[4])
    pair_load.start()

    barrier = pltpu.get_barrier_semaphore()
    for device in (y_dev(1), y_dev(3), x_dev(1), x_dev(3), zc_dev(1), zc_dev(2), zc_dev(6)):
        pl.semaphore_signal(barrier, inc=1, device_id=device, device_id_type=MESH)

    def remote(src, dst, sem, device):
        return pltpu.make_async_remote_copy(
            src_ref=src, dst_ref=dst, send_sem=send_sem.at[sem], recv_sem=recv_sem.at[sem],
            device_id=device, device_id_type=MESH)

    def normalise(raw, buf, raw_first, buf_first, count):
        def step(i, _):
            wide = raw[pl.ds(aligned(raw_first + i * 16, 16), 16), :].astype(F32)
            factor = lax.rsqrt(jnp.sum(wide * wide, axis=1, keepdims=True) + 1e-06)
            buf[pl.ds(aligned(buf_first + i * 16, 16), 16), :] = (wide * factor).astype(BF16)
            return 0
        lax.fori_loop(0, count // 16, step, 0, unroll=4)

    c256 = core * 256
    c128 = core * 128
    src_load.wait()
    normalise(src_raw, src_buf, 0, 0, 256)
    tgt_load.wait()
    normalise(tgt_raw, tgt_buf, c256, c256, 256)
    pl.semaphore_wait(barrier, 7)

    def srow(first, count):
        return src_buf.at[pl.ds(first, count), :]

    def trow(first, count, step=64):
        return tgt_buf.at[pl.ds(aligned(first, step), count), :]

    own_copies = (
        remote(srow(0, 128), srow(256, 128), 0, y_dev(1)),
        remote(srow(128, 128), srow(384, 128), 1, y_dev(3)),
        remote(trow(c256, 128), trow(512 + c256, 128), 2, x_dev(1)),
        remote(trow(c256 + 128, 128), trow(640 + c256, 128), 3, x_dev(3)),
        remote(srow(128, 128), srow(512, 128), 4, y_dev(1)),
        remote(srow(0, 128), srow(640, 128), 5, y_dev(3)),
        remote(trow(c256 + 128, 128), trow(1024 + c256, 128), 6, x_dev(1)),
        remote(trow(c256, 128), trow(1152 + c256, 128), 7, x_dev(3)),
    )
    idx_cols = pl.ds(aligned(c256, 256), 256)
    idx_copies = (
        remote(bwd_hbm.at[:, idx_cols], bwd_raw.at[3, :, idx_cols], 8, x_dev(1)),
        remote(bwd_hbm.at[:, idx_cols], bwd_raw.at[1, :, idx_cols], 9, x_dev(3)),
        remote(bwd_raw.at[3, :, idx_cols], bwd_raw.at[2, :, idx_cols], 10, x_dev(1)),
    )
    for copy in own_copies[:4]:
        copy.start()
    for copy in idx_copies[:2]:
        copy.start()
    for device in (zc_dev(2), zc_dev(6)):
        pl.semaphore_signal(ready_sem, inc=1, device_id=device, device_id_type=MESH)

    normalise(tgt_raw, tgt_buf, 256 - c256, 256 - c256, 256)

    def weight_row(kind, _):
        rel = lax.select(kind < 2, 0, lax.select(kind >= 6, 2, lax.select(kind % 2 == 0, 3, 1)))
        row = 4 * x + lax.rem(y + rel, 4)
        names = [pair_ref[k, row] for k in range(8)]
        for relx in range(4):
            for p in range(2):
                block = 2 * (4 * lax.rem(x + relx, 4) + y) + p
                hit = jnp.int32(0)
                for k in range(8):
                    hit = hit + jnp.where(names[k] == block, 1, 0)
                value = jnp.full((1, 128), jnp.where(hit > 0, 2.0, 0.0), F32)
                for chunk in range(16):
                    if COL_SLOT[chunk] == (relx, p):
                        weight[kind, :, chunk * 128:(chunk + 1) * 128] = value
        return 0

    pair_load.wait()
    lax.fori_loop(0, 8, weight_row, 0)

    lane = lax.broadcasted_iota(I32, (16, 128), 1)

    def far(first, second):
        return jnp.where(lane < 64, first, second), jnp.where(lane < 64, second, first)

    fwd_load.wait()
    fwd_pos[...] = jnp.full((1024, 128), -1, I32)

    def fwd_half(rel, half):
        return fwd_raw[:, pl.ds(aligned(lax.rem(y + rel, 4) * 256 + half * 128, 128), 128)]

    f6, f7 = far(fwd_half(2, 0), fwd_half(2, 1))
    fwd_chunks = (fwd_half(0, 0), fwd_half(0, 1), fwd_half(3, 0), fwd_half(1, 1),
                  fwd_half(3, 1), fwd_half(1, 0), f6, f7)
    for chunk, index in enumerate(fwd_chunks):
        block = index >> 8
        inner = index & 255
        p = block & 1
        rel = ((block >> 3) - x) & 3
        upper = inner >= 128
        near = jnp.where(upper == (rel == 1), 512, jnp.where(rel == 1, 1152, 896))
        quarter = inner >> 6
        distant = jnp.where(quarter == 0, 1536, jnp.where(quarter == 3, 1408,
                            jnp.where(quarter == 2, 1664, 1792))) - p * 128
        base = jnp.where(rel == 0, 0, jnp.where(rel == 2, distant, near))
        column = jnp.where(((block >> 1) & 3) == y, base + p * 256 + inner, -1)
        fwd_pos[chunk * 128:(chunk + 1) * 128, 0:16] = jnp.transpose(column)

    def bwd_rows(index):
        block = index >> 8
        inner = index & 255
        rel = ((block & 3) - y) & 3
        upper = inner >= 128
        near = jnp.where(upper == (rel == 1), 256, jnp.where(rel == 1, 640, 384))
        quarter = inner >> 6
        distant = jnp.where(quarter == 0, 768, jnp.where(quarter == 3, 640,
                            jnp.where(quarter == 2, 768, 896)))
        base = jnp.where(rel == 0, 0, jnp.where(rel == 2, distant, near))
        hit = (block >> 2) == s * 4 + x
        return jnp.where(hit, base + inner, -1)

    def bwd_put(chunk, index):
        bwd_pos[:, chunk * 128:(chunk + 1) * 128] = bwd_rows(index)

    def bwd_half(rel, p, half):
        first = p * 256 + half * 128
        return bwd_raw[rel, :, first:first + 128]

    bwd_load.wait()
    for chunk in range(4):
        bwd_put(chunk, bwd_half(0, chunk // 2, chunk % 2))

    fwd_val[...] = jnp.zeros((1024, 128), F32)
    bwd_val[...] = jnp.zeros((16, 2048), F32)

    def pick_from(part, index, axis):
        other = (1 - axis,)
        numbers = lax.GatherDimensionNumbers(
            offset_dims=(), collapsed_slice_dims=(axis,), start_index_map=(axis,),
            operand_batching_dims=other, start_indices_batching_dims=other)
        return lax.gather(part, index, numbers, (1, 1),
                          mode=lax.GatherScatterMode.PROMISE_IN_BOUNDS)

    def splat(value):
        return lax.full((8, 128), value, I32)

    def split(index, mask, shift):
        pick = lax.bitwise_and(index, splat(mask))
        return lax.expand_dims(pick, (2,)), lax.shift_right_arithmetic(index, splat(shift))

    def region(row, rows, col, cols):
        groups = range(row // 8, (row + rows) // 8)
        for tile in range(col, col + cols, 256):
            scores[row:row + rows, tile:tile + 256] = lax.dot_general(
                src_buf[row:row + rows, :], tgt_buf[tile:tile + 256, :],
                (((1,), (1,)), ((), ())), preferred_element_type=F32)
            chunks = (tile // 128, tile // 128 + 1)
            for chunk in chunks:
                at = slice(chunk * 128, chunk * 128 + 128)
                pick0, where0 = split(bwd_pos[0:8, at], 7, 3)
                pick1, where1 = split(bwd_pos[8:16, at], 7, 3)
                value0, value1 = bwd_val[0:8, at], bwd_val[8:16, at]
                for group in groups:
                    part = scores[group * 8:group * 8 + 8, at]
                    here = splat(group)
                    value0 = lax.select(lax.eq(where0, here), pick_from(part, pick0, 0), value0)
                    value1 = lax.select(lax.eq(where1, here), pick_from(part, pick1, 0), value1)
                bwd_val[0:8, at] = value0
                bwd_val[8:16, at] = value1
            for group in groups:
                at = slice(group * 8, group * 8 + 8)
                pick, where = split(fwd_pos[at, :], 127, 7)
                value = fwd_val[at, :]
                for chunk in chunks:
                    part = scores[at, chunk * 128:chunk * 128 + 128]
                    value = lax.select(lax.eq(where, splat(chunk)), pick_from(part, pick, 1), value)
                fwd_val[at, :] = value

    region(0, 256, 0, 512)
    for copy in own_copies[4:]:
        copy.start()

    for copy in own_copies[:4] + idx_copies[:2]:
        copy.wait_recv()
    idx_copies[2].start()
    far_copies = (
        remote(srow(256, 64), srow(768, 64), 11, y_dev(1)),
        remote(srow(448, 64), srow(832, 64), 12, y_dev(3)),
        remote(trow(512 + c256, 64), trow(1536 + c128, 64), 13, x_dev(1)),
        remote(trow(704 + c256, 64), trow(1600 + c128, 64), 14, x_dev(3)),
        remote(srow(320, 64), srow(960, 64), 15, y_dev(1)),
        remote(srow(384, 64), srow(896, 64), 16, y_dev(3)),
        remote(trow(576 + c256, 64), trow(1856 + c128, 64), 17, x_dev(1)),
        remote(trow(640 + c256, 64), trow(1792 + c128, 64), 18, x_dev(3)),
    )
    for copy in far_copies[:4]:
        copy.start()
    pl.semaphore_wait(ready_sem, 2)
    partner = zc_dev(1)

    def passed(first, count, sem):
        return remote(trow(first, count), trow(first, count), sem, partner)

    def passed_idx(rel, sem):
        piece = bwd_raw.at[rel, :, idx_cols]
        return remote(piece, piece, sem, partner)

    pass_copies = (
        passed(512 + c256, 256, 19), passed(1024 + c256, 256, 20),
        passed(1536 + c128, 64, 21), passed(1600 + c128, 64, 22),
        passed(1856 + c128, 64, 23), passed(1792 + c128, 64, 24),
        passed_idx(3, 25), passed_idx(1, 26), passed_idx(2, 27),
    )
    pass_copies[6].start()
    pass_copies[7].start()
    pass_copies[0].start()
    region(256, 256, 0, 512)
    pass_copies[6].wait_recv()
    pass_copies[7].wait_recv()
    for p in range(2):
        bwd_put(4 + 2 * p, bwd_half(3, p, 0))
        bwd_put(5 + 2 * p, bwd_half(1, p, 1))
        bwd_put(8 + 2 * p, bwd_half(3, p, 1))
        bwd_put(9 + 2 * p, bwd_half(1, p, 0))
    pass_copies[0].wait_recv()
    region(0, 512, 512, 512)
    for copy in far_copies[4:]:
        copy.start()

    for copy in own_copies[4:] + idx_copies[2:]:
        copy.wait_recv()
    pass_copies[1].start()
    pass_copies[8].start()
    region(512, 256, 0, 1024)
    pass_copies[1].wait_recv()
    pass_copies[8].wait_recv()
    for p in range(2):
        near, distant = far(bwd_half(2, p, 0), bwd_half(2, p, 1))
        bwd_put(12 + p, near)
        bwd_put(14 + p, distant)
    region(0, 768, 1024, 512)

    far_copies[2].wait_recv()
    pass_copies[2].start()
    far_copies[3].wait_recv()
    pass_copies[3].start()
    pass_copies[2].wait_recv()
    pass_copies[3].wait_recv()
    region(0, 768, 1536, 256)

    far_copies[6].wait_recv()
    pass_copies[4].start()
    far_copies[7].wait_recv()
    pass_copies[5].start()
    for copy in far_copies[:2] + far_copies[4:6]:
        copy.wait_recv()
    region(768, 256, 0, 1792)
    pass_copies[4].wait_recv()
    pass_copies[5].wait_recv()
    region(0, 1024, 1792, 256)

    lane1 = lane[0:1, :]

    def bwd_sum(chunk):
        return jnp.sum(bwd_val[:, chunk * 128:(chunk + 1) * 128], axis=0, keepdims=True)

    def unfar(first, second):
        if first is None:
            return None, None
        return jnp.where(lane1 < 64, first, second), jnp.where(lane1 < 64, second, first)

    def natural_cols(get):
        blocks = [[None] * 4 for _ in range(4)]
        for chunk in range(4):
            blocks[0][chunk] = get(chunk)
        for p in range(2):
            blocks[3][2 * p] = get(4 + 2 * p)
            blocks[1][2 * p + 1] = get(5 + 2 * p)
            blocks[3][2 * p + 1] = get(8 + 2 * p)
            blocks[1][2 * p] = get(9 + 2 * p)
            blocks[2][2 * p], blocks[2][2 * p + 1] = unfar(get(12 + p), get(14 + p))
        return blocks

    def natural_rows(get):
        blocks = [[None] * 2 for _ in range(4)]
        blocks[0] = [get(0), get(1)]
        blocks[3] = [get(2), get(4)]
        blocks[1] = [get(5), get(3)]
        blocks[2] = list(unfar(get(6), get(7)))
        return blocks

    for rel, rows in enumerate(natural_cols(bwd_sum)):
        for i, value in enumerate(rows):
            bwd_part[lax.rem(x + rel, 4), i:i + 1, :] = value
    bwd_z = [remote(bwd_part, bwd_zin.at[d - 1], 27 + d, zc_dev(d)) for d in range(1, 8)]
    for copy in bwd_z:
        copy.start()

    def to_rows(combine):
        def step(chunk, _):
            at = pl.ds(aligned(chunk * 128, 128), 128)
            rowform[chunk] = combine(jnp.transpose(fwd_val[at, :]))
            return 0
        lax.fori_loop(0, 8, step, 0)

    def row_of(chunk):
        return rowform[chunk]

    to_rows(lambda values: jnp.sum(values[0:16, :], axis=0, keepdims=True))
    for rel, rows in enumerate(natural_rows(row_of)):
        for i, value in enumerate(rows):
            fwd_part[lax.rem(y + rel, 4), i:i + 1, :] = value
    fwd_y = [remote(fwd_part, fwd_in.at[d - 1], 34 + d, y_dev(d)) for d in range(1, 4)]
    for copy in fwd_y:
        copy.start()

    for copy in bwd_z:
        copy.wait_recv()
    total = bwd_part[...]
    for d in range(7):
        total = total + bwd_zin[d]
    bwd_two[...] = total
    bwd_x = [remote(bwd_two, bwd_xin.at[d - 1], 37 + d, x_dev(d)) for d in range(1, 4)]
    for copy in bwd_x:
        copy.start()

    for copy in fwd_y:
        copy.wait_recv()
    frow[...] = (fwd_part[...] + fwd_in[0] + fwd_in[1] + fwd_in[2]) * (1.0 / 16)

    def fwd_mean(rel, half):
        return frow[lax.rem(y + rel, 4), half:half + 1, :]

    m6, m7 = unfar(fwd_mean(2, 0), fwd_mean(2, 1))
    for chunk, row in enumerate((fwd_mean(0, 0), fwd_mean(0, 1), fwd_mean(3, 0), fwd_mean(1, 1),
                                 fwd_mean(3, 1), fwd_mean(1, 0), m6, m7)):
        rowform[chunk] = row

    def spread(chunk, _):
        at = pl.ds(aligned(chunk * 128, 128), 128)
        fcol[at, :] = jnp.transpose(jnp.broadcast_to(rowform[chunk], (128, 128)))
        return 0

    lax.fori_loop(0, 8, spread, 0)

    for copy in bwd_x:
        copy.wait_recv()
    bwd_two2 = (bwd_two[...] + bwd_xin[0] + bwd_xin[1] + bwd_xin[2]) * (1.0 / 16)
    bwd_part2 = tgt_part
    bwd_part2[...] = bwd_two2

    def bwd_mean(rel, i):
        return bwd_part2[lax.rem(x + rel, 4), i:i + 1, :]

    def put_brow(chunk, value):
        brow[:, chunk * 128:(chunk + 1) * 128] = value

    for chunk in range(4):
        put_brow(chunk, bwd_mean(0, chunk))
    for p in range(2):
        put_brow(4 + 2 * p, bwd_mean(3, 2 * p))
        put_brow(5 + 2 * p, bwd_mean(1, 2 * p + 1))
        put_brow(8 + 2 * p, bwd_mean(3, 2 * p + 1))
        put_brow(9 + 2 * p, bwd_mean(1, 2 * p))
        near, distant = unfar(bwd_mean(2, 2 * p), bwd_mean(2, 2 * p + 1))
        put_brow(12 + p, near)
        put_brow(14 + p, distant)

    def margins(chunks, unroll, first):
        def margin_rows(step, peaks):
            peaks = list(peaks)
            kind = step // (16 // unroll)
            for g in range(unroll):
                at = pl.ds(aligned(step * (8 * unroll) + g * 8, 8), 8)
                mean = fcol[at, :]
                best = jnp.zeros((8, 128), F32) if first else fwd_val[at, :]
                for i, chunk in enumerate(chunks):
                    cols = slice(chunk * 128, (chunk + 1) * 128)
                    margin = (scores[at, cols] * weight[kind, :, cols]) / (mean + brow[:, cols])
                    best = jnp.maximum(best, margin)
                    peaks[i] = jnp.maximum(peaks[i], margin)
                fwd_val[at, :] = best
            return tuple(peaks)

        peaks = lax.fori_loop(0, 128 // unroll, margin_rows,
                              (jnp.zeros((8, 128), F32),) * len(chunks))
        return {chunk: jnp.max(peak, axis=0, keepdims=True) for chunk, peak in zip(chunks, peaks)}

    def put_peaks(peaks):
        for rel, rows in enumerate(natural_cols(peaks.get)):
            for i, value in enumerate(rows):
                if value is not None:
                    tgt_part[lax.rem(x + rel, 4), i:i + 1, :] = value

    put_peaks(margins(range(4, 16), 4, True))
    def tgt_send(piece, dx, dz):
        device = (2 * lax.rem(z + dz, 4) + core, 4 * lax.rem(x + dx, 4) + y)
        place = 4 * dx + dz - 1
        return remote(piece, tgt_in.at[place], 41 + place, device)

    tgt_copies = [tgt_send(tgt_part.at[lax.rem(x + dx, 4)], dx, dz)
                  for dz in range(4) for dx in (2, 1, 3)]
    for copy in tgt_copies:
        copy.start()
    for chunk, value in margins(range(4), 8, False).items():
        tgt_own[chunk:chunk + 1, :] = value
    own_sends = [tgt_send(tgt_own, 0, dz) for dz in (2, 1, 3)]
    for copy in own_sends:
        copy.start()
    tgt_copies += own_sends

    to_rows(lambda values: jnp.max(values, axis=0, keepdims=True))
    for rel, rows in enumerate(natural_rows(row_of)):
        for i, value in enumerate(rows):
            src_part[lax.rem(y + rel, 4), i:i + 1, :] = value
    src_y = [remote(src_part.at[lax.rem(y + d, 4)], src_in.at[d - 1], 56 + d, y_dev(d))
             for d in range(1, 4)]
    for copy in src_y:
        copy.start()

    for copy in tgt_copies:
        copy.wait_recv()
    best = tgt_own[...]
    for place in range(15):
        best = jnp.maximum(best, tgt_in[place])
    tgt_two[...] = best
    tgt_core = remote(tgt_two, tgt_other, 56, partner)
    tgt_core.start()
    for copy in src_y:
        copy.wait_recv()
    src_out[...] = jnp.maximum(jnp.maximum(src_part[y], src_in[0]),
                               jnp.maximum(src_in[1], src_in[2]))
    tgt_core.wait_recv()
    tgt_out[...] = jnp.maximum(best, tgt_other[...])

    for copies in (own_copies, idx_copies, far_copies, pass_copies, bwd_z, fwd_y, bwd_x,
                   tgt_copies, src_y, (tgt_core,)):
        for copy in copies:
            copy.wait_send()


def body(src_emb, tgt_emb, pair_list, fwd_idx, bwd_idx):
    hbm = pl.BlockSpec(memory_space=pl.ANY)
    vmem = pl.BlockSpec(memory_space=pltpu.VMEM)
    src_best, tgt_best = pl.pallas_call(
        kernel,
        out_shape=(jax.ShapeDtypeStruct((2, 128), F32), jax.ShapeDtypeStruct((4, 128), F32)),
        in_specs=[hbm] * 5,
        out_specs=(vmem, vmem),
        scratch_shapes=[
            pltpu.SMEM((8, 16), I32),
            pltpu.VMEM((256, D), BF16), pltpu.VMEM((512, D), BF16),
            pltpu.VMEM((1024, D), BF16), pltpu.VMEM((2048, D), BF16),
            pltpu.VMEM((1024, 2048), F32),
            pltpu.VMEM((16, 1024), I32), pltpu.VMEM((4, 16, 512), I32),
            pltpu.VMEM((1024, 128), I32), pltpu.VMEM((16, 2048), I32),
            pltpu.VMEM((1024, 128), F32), pltpu.VMEM((16, 2048), F32),
            pltpu.VMEM((8, 1, 2048), F32),
            pltpu.VMEM((4, 2, 128), F32), pltpu.VMEM((8, 1, 128), F32), pltpu.VMEM((1024, 128), F32),
            pltpu.VMEM((1, 2048), F32),
            pltpu.VMEM((4, 2, 128), F32), pltpu.VMEM((3, 4, 2, 128), F32),
            pltpu.VMEM((4, 4, 128), F32), pltpu.VMEM((7, 4, 4, 128), F32),
            pltpu.VMEM((4, 4, 128), F32), pltpu.VMEM((3, 4, 4, 128), F32),
            pltpu.VMEM((4, 2, 128), F32), pltpu.VMEM((3, 2, 128), F32),
            pltpu.VMEM((4, 4, 128), F32), pltpu.VMEM((4, 128), F32),
            pltpu.VMEM((15, 4, 128), F32), pltpu.VMEM((4, 128), F32), pltpu.VMEM((4, 128), F32),
            pltpu.SemaphoreType.DMA((5,)),
            pltpu.SemaphoreType.DMA((60,)), pltpu.SemaphoreType.DMA((60,)),
            pltpu.SemaphoreType.REGULAR,
        ],
        compiler_params=pltpu.CompilerParams(
            collective_id=0, has_side_effects=True, vmem_limit_bytes=60 << 20),
    )(src_emb, tgt_emb, pair_list.T, fwd_idx.T, bwd_idx.T)

    def flatten(src_ref, tgt_ref, src_flat, tgt_flat):
        src_flat[...] = src_ref[...].reshape(256)
        tgt_flat[...] = tgt_ref[...].reshape(512)

    return pl.pallas_call(
        flatten,
        out_shape=(jax.ShapeDtypeStruct((256,), F32), jax.ShapeDtypeStruct((512,), F32)),
        in_specs=[vmem, vmem],
        out_specs=(vmem, vmem),
    )(src_best, tgt_best)


def solution(mesh):
    return jax.shard_map(
        body,
        mesh=mesh,
        in_specs=(
            P(("src", "tgt"), None),
            P("tgt", None),
            P("src", None),
            P("src", None),
            P("tgt", None),
        ),
        out_specs=(P(("src", "tgt")), P("tgt")),
        check_vma=False,
    )
```
